32 devices in a mesh: dp: 32 (over z, y, x, core).
Axes of the slice: x: 2, y: 2, z: 4, core: 2. Of those that a mesh axis runs over, the one named last changes fastest.
Arguments:
- grads: bfloat16 [64, 1024, 1024], P('dp'), may hold values from -6 to 6
- memory: bfloat16 [64, 1024, 1024], P('dp'), may hold values from -6 to 6
- block_ids: int32 [16], replicated, may hold values from 0 to 63, as said below
- layer_ids: int32 [16], replicated, may hold values from 0 to 1, as said below
- master: float32 [128, 16384], P(None, 'dp'), may hold values from -8 to 8
- first_moment: float32 [128, 16384], P(None, 'dp'), may hold values from -8 to 8
- second_moment: float32 [128, 16384], P(None, 'dp'), may hold values from 0.25 to 4
Outputs:
- new_memory: bfloat16 [64, 1024, 1024], P('dp')
- master_new: float32 [128, 16384], P(None, 'dp')
- first_new: float32 [128, 16384], P(None, 'dp')
- second_new: float32 [128, 16384], P(None, 'dp')
- step_blocks: bfloat16 [16, 16384], replicated
The draws below stay inside these ranges and needn't reach their ends.
Inputs may be any that keep to these rules, and one draw needn't show every extreme that they name: Block ids number the 64 tiles of a layer, and the pairs (layer_ids[k], block_ids[k]) are distinct. `layer_ids`: every layer is named by at least a quarter of the 16 entries, rounded down.
All inputs are finite; a program needn't handle non-finite values.
Results may differ from the reference program's by a relative error of at most 0.0004.
Values may be sent and summed in bfloat16 or wider, within the bound.
A program may use at most 64 MiB of HBM per device.

```python
import math
import jax
import jax.numpy as jnp
from jax import lax

D = 1024
LAYERS = 2
TILE = 128
SEL = 16
BLOCKS_LAYER = 64
BLOCKS = 128
TILE_ENT = 16384
N_DP = 32


def pick_entries(key):
    folded = jax.random.fold_in(key, 7)
    key_count, key_first, key_second, key_shuffle = jax.random.split(folded, 4)
    least = SEL // 4
    count_first = jax.random.randint(key_count, (), least, SEL - least + 1)
    first_perm = jax.random.permutation(key_first, BLOCKS_LAYER)[:SEL]
    second_perm = jax.random.permutation(key_second, BLOCKS_LAYER)[:SEL]
    position = jnp.arange(SEL, dtype=jnp.int32)
    layer_list = (position >= count_first).astype(jnp.int32)
    later_index = jnp.clip(position - count_first, 0, SEL - 1)
    block_list = jnp.where(layer_list == 0, first_perm[position], second_perm[later_index]).astype(jnp.int32)
    shuffle = jax.random.permutation(key_shuffle, SEL)
    return (layer_list[shuffle], block_list[shuffle])


def draw_block_ids(key, part):
    return pick_entries(key)[1]


def draw_layer_ids(key, part):
    return pick_entries(key)[0]


def rising_field(key):
    entry_row = (jnp.arange(TILE_ENT) // TILE).astype(jnp.float32)
    factor = 1.0 + 2.0 * entry_row / (TILE - 1)
    normal_part = jnp.clip(jax.random.normal(key, (BLOCKS, TILE_ENT), jnp.float32), -4.0, 4.0)
    return normal_part * factor[None, :] * 0.5


def draw_master(key, part):
    return rising_field(jax.random.fold_in(key, 11))


def draw_first_moment(key, part):
    return rising_field(jax.random.fold_in(key, 23))


def shard_levels(key, shape, shards, smallest, high):
    def one(axis_at, parts):
        heights = jax.random.uniform(jax.random.fold_in(jax.random.fold_in(key, 6), axis_at), (parts,), jnp.float32, smallest / len(shards), high / len(shards))
        return jnp.repeat(jnp.exp(heights), shape[axis_at] // parts).reshape((-1,) + (1,) * (len(shape) - axis_at - 1))

    gain = one(*shards[0])
    for cut in shards[1:]:
        gain = gain * one(*cut)
    return gain


def scatter_about(rng, extent, deviation, limit, cuts=(), kind=jnp.bfloat16):
    loudness = shard_levels(rng, extent, cuts, -0.22, 0.18) if cuts else 1.0
    entries = jax.random.normal(rng, extent, jnp.float32) * deviation * loudness
    return jnp.minimum(jnp.maximum(entries, -limit), limit).astype(kind)


def setup_inputs(seed: int = 0) -> dict:
    seeds = jax.random.split(jax.random.key(seed), 8)
    return {
        "grads": scatter_about(seeds[0], (N_DP * LAYERS, D, D), 0.5, 6.0, ((0, 32),)),
        "memory": scatter_about(seeds[1], (N_DP * LAYERS, D, D), 0.5, 6.0, ((0, 32),)),
        "block_ids": draw_block_ids(jax.random.fold_in(seeds[7], 71), 0),
        "layer_ids": draw_layer_ids(jax.random.fold_in(seeds[7], 71), 0),
        "master": draw_master(jax.random.fold_in(seeds[7], 71), 0),
        "first_moment": draw_first_moment(jax.random.fold_in(seeds[7], 71), 0),
        "second_moment": jnp.clip(jnp.exp(math.log(4.0) - 2.7725887 * jax.random.uniform(seeds[6], (BLOCKS, TILE_ENT), jnp.float32) ** shard_levels(seeds[6], (BLOCKS, TILE_ENT), ((1, 32),), -0.2, 0.2)), 0.25, 4.0),
    }


filter_rate = 0.3
beta_one = 0.9
beta_two = 0.999
adam_eps = 1e-06
weight_decay = 0.01
learn_rate = 0.01
norm_eps = 1e-06

def take_tiles(source, layer_ids, tile_row, tile_col):

    def single(layer_id, row_tile, col_tile):
        return lax.dynamic_slice(source, (layer_id, row_tile * TILE, col_tile * TILE), (1, TILE, TILE))[0]
    return jax.vmap(single)(layer_ids, tile_row, tile_col)

def pack_blocks(grads_dev, memory_dev, layer_ids, tile_row, tile_col):
    grad_tiles = take_tiles(grads_dev, layer_ids, tile_row, tile_col).astype(jnp.float32)
    memory_tiles = take_tiles(memory_dev, layer_ids, tile_row, tile_col).astype(jnp.float32)
    combined = grad_tiles + memory_tiles
    return combined.reshape(combined.shape[0], TILE * TILE)

def selected_mask(layer_ids, block_ids, layers, tile_count):
    columns = layer_ids * (tile_count * tile_count) + block_ids
    all_columns = jnp.arange(layers * tile_count * tile_count, dtype=jnp.int32)
    chosen = jnp.any(columns[:, None] == all_columns[None, :], axis=0)
    return chosen.reshape(layers, tile_count, 1, tile_count, 1)

def filter_memory(grads_dev, memory_dev, chosen):
    layers, model_width, _ = grads_dev.shape
    tile_count = model_width // TILE
    accumulated = grads_dev.astype(jnp.float32) + memory_dev.astype(jnp.float32)
    shaped = accumulated.reshape(layers, tile_count, TILE, tile_count, TILE)
    filtered = jnp.where(chosen, jnp.float32(0.0), shaped).reshape(layers, model_width, model_width)
    mixed = (1.0 - filter_rate) * memory_dev.astype(jnp.float32) + filter_rate * filtered
    return mixed.astype(jnp.bfloat16)

def adam_rows(summed, weights_sel, first_old, second_old):
    first_sel = beta_one * first_old + (1.0 - beta_one) * summed
    second_sel = beta_two * second_old + (1.0 - beta_two) * summed * summed
    update = first_sel / (jnp.sqrt(second_sel) + adam_eps) + weight_decay * weights_sel
    return (first_sel, second_sel, update)

def layer_squares(member, values):
    return lax.optimization_barrier(jnp.sum(member * lax.optimization_barrier(jnp.sum(values * values, axis=1))[:, None], axis=0))

def trust_rows(member, weight_total, update_total):
    trust_ratio = jnp.sqrt(weight_total / (update_total + norm_eps))
    return lax.optimization_barrier(jnp.sum(member * trust_ratio[None, :], axis=1))

def reference(grads, memory, block_ids, layer_ids, master, first_moment, second_moment):
    tile_count = D // TILE
    tile_row = block_ids // tile_count
    tile_col = block_ids % tile_count
    chosen = selected_mask(layer_ids, block_ids, LAYERS, tile_count)
    grads_view = grads.reshape(N_DP, LAYERS, D, D)
    memory_view = memory.reshape(N_DP, LAYERS, D, D)

    def per_device(running, arrays):
        grads_dev, memory_dev = arrays
        packed = pack_blocks(grads_dev, memory_dev, layer_ids, tile_row, tile_col)
        return (running + packed, filter_memory(grads_dev, memory_dev, chosen))
    summed, filtered_all = lax.scan(per_device, jnp.zeros((SEL, TILE * TILE), jnp.float32), (grads_view, memory_view))
    new_memory = filtered_all.reshape(N_DP * LAYERS, D, D)
    columns = layer_ids * BLOCKS_LAYER + block_ids
    weights_sel = jnp.take(master, columns, axis=0)
    first_old = jnp.take(first_moment, columns, axis=0)
    second_old = jnp.take(second_moment, columns, axis=0)
    first_sel, second_sel, update = adam_rows(summed, weights_sel, first_old, second_old)
    member = (layer_ids[:, None] == jnp.arange(LAYERS, dtype=jnp.int32)[None, :]).astype(jnp.float32)
    row_ratio = trust_rows(member, layer_squares(member, weights_sel), layer_squares(member, update))
    scaled = row_ratio[:, None] * update
    step_blocks = scaled.astype(jnp.bfloat16)
    master_new = master.at[columns].set(weights_sel - learn_rate * scaled)
    first_new = first_moment.at[columns].set(first_sel)
    second_new = second_moment.at[columns].set(second_sel)
    return (new_memory, master_new, first_new, second_new, step_blocks)
```

```python
import functools

import jax
import jax.numpy as jnp
from jax import lax
from jax.experimental import pallas as pl
from jax.experimental.pallas import tpu as pltpu
from jax.sharding import PartitionSpec as P

TILE = 128


filter_rate = 0.3
beta_one = 0.9
beta_two = 0.999
adam_eps = 1e-06
weight_decay = 0.01
learn_rate = 0.01
norm_eps = 1e-06


def take_tiles(source, layer_ids, tile_row, tile_col):

    def single(layer_id, row_tile, col_tile):
        return lax.dynamic_slice(
            source, (layer_id, row_tile * TILE, col_tile * TILE), (1, TILE, TILE)
        )[0]

    return jax.vmap(single)(layer_ids, tile_row, tile_col)


def pack_blocks(grads_dev, memory_dev, layer_ids, tile_row, tile_col):
    grad_tiles = take_tiles(grads_dev, layer_ids, tile_row, tile_col).astype(jnp.float32)
    memory_tiles = take_tiles(memory_dev, layer_ids, tile_row, tile_col).astype(jnp.float32)
    combined = grad_tiles + memory_tiles
    return combined.reshape(combined.shape[0], TILE * TILE)


def selected_mask(layer_ids, block_ids, layers, tile_count):
    columns = layer_ids * (tile_count * tile_count) + block_ids
    all_columns = jnp.arange(layers * tile_count * tile_count, dtype=jnp.int32)
    chosen = jnp.any(columns[:, None] == all_columns[None, :], axis=0)
    return chosen.reshape(layers, tile_count, 1, tile_count, 1)


def filter_memory(grads_dev, memory_dev, chosen):
    layers, model_width, _ = grads_dev.shape
    tile_count = model_width // TILE
    accumulated = grads_dev.astype(jnp.float32) + memory_dev.astype(jnp.float32)
    shaped = accumulated.reshape(layers, tile_count, TILE, tile_count, TILE)
    filtered = jnp.where(chosen, jnp.float32(0.0), shaped).reshape(layers, model_width, model_width)
    mixed = (1.0 - filter_rate) * memory_dev.astype(jnp.float32) + filter_rate * filtered
    return mixed.astype(jnp.bfloat16)


def adam_rows(summed, weights_sel, first_old, second_old):
    first_sel = beta_one * first_old + (1.0 - beta_one) * summed
    second_sel = beta_two * second_old + (1.0 - beta_two) * summed * summed
    update = first_sel / (jnp.sqrt(second_sel) + adam_eps) + weight_decay * weights_sel
    return (first_sel, second_sel, update)


def layer_squares(member, values):
    return jnp.sum(member * jnp.sum(values * values, axis=1)[:, None], axis=0)


def trust_rows(member, weight_total, update_total):
    trust_ratio = jnp.sqrt(weight_total / (update_total + norm_eps))
    return jnp.sum(member * trust_ratio[None, :], axis=1)


def on_device(grads, memory, block_ids, layer_ids, master, first_moment, second_moment):
    layers, model_width, _ = grads.shape
    tile_count = model_width // TILE
    tile_row = block_ids // tile_count
    tile_col = block_ids % tile_count
    columns = layer_ids * (tile_count * tile_count) + block_ids
    member = (layer_ids[:, None] == jnp.arange(layers, dtype=jnp.int32)[None, :]).astype(
        jnp.float32
    )
    weights_sel = jnp.take(master, columns, axis=0)
    first_old = jnp.take(first_moment, columns, axis=0)
    second_old = jnp.take(second_moment, columns, axis=0)
    packed = pack_blocks(grads, memory, layer_ids, tile_row, tile_col)
    summed = lax.psum_scatter(packed, "dp", scatter_dimension=1, tiled=True)
    first_sel, second_sel, update = adam_rows(summed, weights_sel, first_old, second_old)
    weight_total, update_total = lax.psum(
        (layer_squares(member, weights_sel), layer_squares(member, update)), "dp"
    )
    scaled = trust_rows(member, weight_total, update_total)[:, None] * update
    step_blocks = lax.all_gather(scaled.astype(jnp.bfloat16), "dp", axis=1, tiled=True)
    new_memory = filter_memory(
        grads, memory, selected_mask(layer_ids, block_ids, layers, tile_count)
    )
    master_new = master.at[columns].set(weights_sel - learn_rate * scaled)
    first_new = first_moment.at[columns].set(first_sel)
    second_new = second_moment.at[columns].set(second_sel)
    return (new_memory, master_new, first_new, second_new, step_blocks)


def xor_bit(bit, flip):
    return bit if flip == 0 else 1 - bit


def pack_kernel(layers_smem, blocks_smem, grads_ref, memory_ref, master_ref, first_ref, second_ref,
                out_ref, packed_ref, state_ref, member_ref):
    layer, row = pl.program_id(0), pl.program_id(1)
    tile_count = pl.num_programs(1)
    count = layers_smem.shape[0]
    layers = member_ref.shape[0]
    pieces = state_ref.shape[1] // count

    @pl.when((layer == 0) & (row == 0))
    def _():
        for k in range(count):
            column = layers_smem[k] * (tile_count * tile_count) + blocks_smem[k]
            for s, ref in enumerate((master_ref, first_ref, second_ref)):
                line = ref[pl.ds(column, 1), :]
                for j in range(pieces):
                    state_ref[s, j * count + k:j * count + k + 1, :] = line[:, j * TILE:(j + 1) * TILE]
            for l in range(layers):
                flag = jnp.where(layers_smem[k] == l, jnp.float32(1.0), jnp.float32(0.0))
                for j in range(pieces):
                    member_ref[l, j * count + k:j * count + k + 1, :] = jnp.full((1, TILE), flag, jnp.float32)

    memory = memory_ref[0].astype(jnp.float32)
    total = grads_ref[0].astype(jnp.float32) + memory
    out_ref[0] = ((1.0 - filter_rate) * memory + filter_rate * total).astype(out_ref.dtype)
    for k in range(count):
        block = blocks_smem[k]

        @pl.when((layers_smem[k] == layer) & (lax.div(block, tile_count) == row))
        def _():
            lanes = pl.ds(pl.multiple_of(lax.rem(block, tile_count) * TILE, TILE), TILE)
            kept = memory_ref[0, :, lanes].astype(jnp.float32)
            packed_ref[pl.ds(k, TILE, stride=count), :] = grads_ref[0, :, lanes].astype(jnp.float32) + kept
            out_ref[0, :, lanes] = ((1.0 - filter_rate) * kept).astype(out_ref.dtype)


def exchange_kernel(n, packed_ref, state_ref, member_ref, rows_ref, step_ref,
                    recv1, send2, recv2, send3, recv3, stat_own, stat_in, stat_mid, stat_far,
                    s1, r1, s2, r2, s3, r3, s4, r4, s5, r5, sz, sp, sc, rg):
    depth = n // 8
    layers = member_ref.shape[0]
    count = step_ref.shape[0]
    entries = step_ref.shape[1] // n
    pieces = entries // TILE
    me = lax.axis_index("dp")
    core = lax.rem(me, 2)
    x = lax.rem(lax.div(me, 2), 2)
    y = lax.rem(lax.div(me, 4), 2)
    z = lax.div(me, 8)

    def device(dz, dq, dc, back=False):
        far = lax.rem(z + (depth - dz if back else dz), depth) if dz else z
        return far * 8 + xor_bit(y, dq // 2) * 4 + xor_bit(x, dq % 2) * 2 + xor_bit(core, dc)

    def plane(dq):
        return xor_bit(y, dq // 2) * 2 + xor_bit(x, dq % 2)

    def copy(src, dst, send, recv, peer):
        return pltpu.make_async_remote_copy(
            src_ref=src, dst_ref=dst, send_sem=send, recv_sem=recv,
            device_id=(peer,), device_id_type=pl.DeviceIdType.MESH)

    barrier = pltpu.get_barrier_semaphore()
    peers = [device(0, i // 2, i % 2) for i in range(1, 8)] + [device(dz, 0, 0) for dz in range(1, depth)]
    for peer in peers:
        pl.semaphore_signal(barrier, inc=1, device_id=(peer,), device_id_type=pl.DeviceIdType.MESH)
    pl.semaphore_wait(barrier, len(peers))

    order = (3, 1, 2, 0)
    first_hop = {}
    for dq in order:
        first_hop[dq] = copy(packed_ref.at[:, plane(dq), 1 - core], recv1.at[dq], s1.at[dq], r1.at[dq], device(0, 0, 1))
        first_hop[dq].start()
    second_hop = []
    for dq in order[:3]:
        first_hop[dq].wait_recv()
        send2[dq - 1] = packed_ref[:, plane(dq), core] + recv1[dq]
        hop = copy(send2.at[dq - 1], recv2.at[dq - 1], s2.at[dq - 1], r2.at[dq - 1], device(0, dq, 0))
        hop.start()
        second_hop.append(hop)
    first_hop[0].wait_recv()
    for hop in second_hop:
        hop.wait_recv()
    here = plane(0)

    def plane_sum(at):
        return (packed_ref[at, here, core] + recv1[0, at]) + ((recv2[0, at] + recv2[1, at]) + recv2[2, at])

    third_hop = []
    for dz in range(1, depth):
        send3[dz - 1] = plane_sum(lax.rem(z + dz, depth))
        hop = copy(send3.at[dz - 1], recv3.at[dz - 1], s3.at[dz - 1], r3.at[dz - 1], device(dz, 0, 0))
        hop.start()
        third_hop.append(hop)
    summed = plane_sum(z)
    for dz in range(1, depth):
        third_hop[dz - 1].wait_recv()
        summed = summed + recv3[dz - 1]

    weights = state_ref[0]
    first_sel = beta_one * state_ref[1] + (1.0 - beta_one) * summed
    second_sel = beta_two * state_ref[2] + (1.0 - beta_two) * summed * summed
    update = first_sel / (jnp.sqrt(second_sel) + adam_eps) + weight_decay * weights
    rows_ref[1] = first_sel
    rows_ref[2] = second_sel
    stat_own[...] = jnp.zeros_like(stat_own)
    for l in range(layers):
        member = member_ref[l]
        stat_own[l:l + 1, :] = jnp.sum(member * (weights * weights), axis=0, keepdims=True)
        stat_own[layers + l:layers + l + 1, :] = jnp.sum(member * (update * update), axis=0, keepdims=True)
    near = []
    for i in range(1, 8):
        hop = copy(stat_own, stat_in.at[i - 1], s4.at[i - 1], r4.at[i - 1], device(0, i // 2, i % 2))
        hop.start()
        near.append(hop)
    total = stat_own[...]
    for i in range(1, 8):
        near[i - 1].wait_recv()
        total = total + stat_in[i - 1]
    stat_mid[...] = total
    away = []
    for dz in range(1, depth):
        hop = copy(stat_mid, stat_far.at[dz - 1], s5.at[dz - 1], r5.at[dz - 1], device(dz, 0, 0))
        hop.start()
        away.append(hop)
    for dz in range(1, depth):
        away[dz - 1].wait_recv()
        total = total + stat_far[dz - 1]
    sums = jnp.sum(total, axis=1, keepdims=True)
    factor = jnp.zeros_like(update)
    for l in range(layers):
        ratio = jnp.sqrt(sums[l:l + 1] / (sums[layers + l:layers + l + 1] + norm_eps))
        factor = factor + member_ref[l] * ratio
    scaled = factor * update
    for j in range(pieces):
        lanes = pl.ds(pl.multiple_of(me * entries + j * TILE, TILE), TILE)
        step_ref[:, lanes] = scaled[j * count:(j + 1) * count].astype(step_ref.dtype)

    def chunk(dz, dq, dc):
        return step_ref.at[:, pl.ds(pl.multiple_of(device(dz, dq, dc, back=True) * entries, TILE), entries)]

    started = list(near) + list(away) + second_hop + third_hop + list(first_hop.values())

    def forward(dz, dq, dc, to_z, to_q, to_c, send, there):
        block = chunk(dz, dq, dc)
        hop = copy(block, block, send, rg.at[there], device(to_z, to_q, to_c))
        hop.start()
        started.append(hop)

    def arrived(dz, dq, dc):
        block = chunk(dz, dq, dc)
        at = (dz * 4 + dq) * 2 + dc
        copy(block, block, sz.at[0], rg.at[at], device(0, 0, 1)).wait_recv()

    def spread(dz):
        for dq in order[:3]:
            forward(dz, 0, 0, 0, dq, 0, sp.at[dz * 3 + dq - 1], (dz * 4 + dq) * 2)

    def hand_over(dz, dq):
        forward(dz, dq, 0, 0, 0, 1, sc.at[dz * 4 + dq], (dz * 4 + dq) * 2 + 1)

    for dz in range(1, depth):
        forward(0, 0, 0, dz, 0, 0, sz.at[dz - 1], dz * 8)
    spread(0)
    hand_over(0, 0)
    rows_ref[0] = weights - learn_rate * scaled
    reach = sorted(range(1, depth), key=lambda dz: min(dz, depth - dz))
    for at, dz in enumerate(reach):
        arrived(dz, 0, 0)
        spread(dz)
        hand_over(dz, 0)
    for dz in [0] + reach:
        for dq in (1, 2, 3):
            arrived(dz, dq, 0)
            hand_over(dz, dq)
    for dz in range(depth):
        for dq in range(4):
            arrived(dz, dq, 1)
    for hop in started:
        hop.wait_send()


def state_kernel(layers_smem, blocks_smem, rows_ref, master_ref, first_ref, second_ref,
                 master_out, first_out, second_out, *, layer_rows):
    count = layers_smem.shape[0]
    pieces = rows_ref.shape[1] // count
    outs = ((master_ref, master_out), (first_ref, first_out), (second_ref, second_out))
    for old, new in outs:
        new[...] = old[...]
    for k in range(count):
        column = layers_smem[k] * layer_rows + blocks_smem[k]
        base = pl.ds(pl.multiple_of(lax.div(column, 8) * 8, 8), 8)
        hit = lax.broadcasted_iota(jnp.int32, (8, TILE), 0) == lax.rem(column, 8)
        for s, (_, new) in enumerate(outs):
            for j in range(pieces):
                lanes = slice(j * TILE, (j + 1) * TILE)
                line = rows_ref[s, j * count + k:j * count + k + 1, :]
                new[base, lanes] = jnp.where(hit, line, new[base, lanes])


def on_device_kernels(n, grads, memory, block_ids, layer_ids, master, first_moment, second_moment):
    layers, width, _ = grads.shape
    tile_count = width // TILE
    count = block_ids.shape[0]
    entries = master.shape[1]
    lines = entries // TILE * count
    depth = n // 8
    f32 = jnp.float32
    slab = pl.BlockSpec((1, TILE, width), lambda l, r, a, b: (l, r, 0))
    whole = lambda shape: pl.BlockSpec(shape, lambda l, r, a, b: (0,) * len(shape))
    new_memory, packed, state, member = pl.pallas_call(
        pack_kernel,
        grid_spec=pltpu.PrefetchScalarGridSpec(
            num_scalar_prefetch=2, grid=(layers, tile_count),
            in_specs=[slab, slab] + [whole(master.shape)] * 3,
            out_specs=[slab, whole((n * lines, TILE)), whole((3, lines, TILE)), whole((layers, lines, TILE))]),
        out_shape=[
            jax.ShapeDtypeStruct(memory.shape, jnp.bfloat16),
            jax.ShapeDtypeStruct((n * lines, TILE), f32),
            jax.ShapeDtypeStruct((3, lines, TILE), f32),
            jax.ShapeDtypeStruct((layers, lines, TILE), f32)],
        name="pack",
    )(layer_ids, block_ids, grads, memory, master, first_moment, second_moment)
    vmem = pl.BlockSpec(memory_space=pltpu.VMEM)
    stat_rows = -(-2 * layers // 8) * 8
    dma = pltpu.SemaphoreType.DMA
    rows, step_blocks = pl.pallas_call(
        functools.partial(exchange_kernel, n),
        out_shape=[jax.ShapeDtypeStruct((3, lines, TILE), f32),
                   jax.ShapeDtypeStruct((count, n * entries), jnp.bfloat16)],
        in_specs=[vmem] * 3,
        out_specs=[vmem] * 2,
        scratch_shapes=[
            pltpu.VMEM((4, depth, lines, TILE), f32),
            pltpu.VMEM((3, depth, lines, TILE), f32),
            pltpu.VMEM((3, depth, lines, TILE), f32),
            pltpu.VMEM((depth - 1, lines, TILE), f32),
            pltpu.VMEM((depth - 1, lines, TILE), f32),
            pltpu.VMEM((stat_rows, TILE), f32),
            pltpu.VMEM((7, stat_rows, TILE), f32),
            pltpu.VMEM((stat_rows, TILE), f32),
            pltpu.VMEM((depth - 1, stat_rows, TILE), f32),
            dma((4,)), dma((4,)), dma((3,)), dma((3,)), dma((depth - 1,)), dma((depth - 1,)),
            dma((7,)), dma((7,)), dma((depth - 1,)), dma((depth - 1,)),
            dma((depth - 1,)), dma((depth * 3,)), dma((depth * 4,)), dma((n,))],
        compiler_params=pltpu.CompilerParams(collective_id=0, has_side_effects=True),
        name="exchange",
    )(packed.reshape(depth, 4, 2, lines, TILE), state, member)
    smem = pl.BlockSpec(memory_space=pltpu.SMEM)
    like = jax.ShapeDtypeStruct(master.shape, f32)
    master_new, first_new, second_new = pl.pallas_call(
        functools.partial(state_kernel, layer_rows=tile_count * tile_count),
        out_shape=[like] * 3,
        in_specs=[smem, smem] + [vmem] * 4,
        out_specs=[vmem] * 3,
        name="state",
    )(layer_ids, block_ids, rows, master, first_moment, second_moment)
    return (new_memory, master_new, first_new, second_new, step_blocks)


def solution(mesh):
    n = mesh.shape["dp"]

    def body(*args):
        entries, count = args[4].shape[1], args[2].shape[0]
        if n % 8 == 0 and n > 8 and entries % TILE == 0 and count % 16 == 0:
            return on_device_kernels(n, *args)
        return on_device(*args)

    in_specs = (
        P("dp", None, None),
        P("dp", None, None),
        P(),
        P(),
        P(None, "dp"),
        P(None, "dp"),
        P(None, "dp"),
    )
    out_specs = (P("dp", None, None), P(None, "dp"), P(None, "dp"), P(None, "dp"), P())
    return jax.shard_map(
        body, mesh=mesh, in_specs=in_specs, out_specs=out_specs, check_vma=False
    )
```

```python
import functools

import jax
import jax.numpy as jnp
from jax import lax
from jax.experimental import pallas as pl
from jax.experimental.pallas import tpu as pltpu
from jax.sharding import PartitionSpec as P

TILE = 128


filter_rate = 0.3
beta_one = 0.9
beta_two = 0.999
adam_eps = 1e-06
weight_decay = 0.01
learn_rate = 0.01
norm_eps = 1e-06


def take_tiles(source, layer_ids, tile_row, tile_col):

    def single(layer_id, row_tile, col_tile):
        return lax.dynamic_slice(
            source, (layer_id, row_tile * TILE, col_tile * TILE), (1, TILE, TILE)
        )[0]

    return jax.vmap(single)(layer_ids, tile_row, tile_col)


def pack_blocks(grads_dev, memory_dev, layer_ids, tile_row, tile_col):
    grad_tiles = take_tiles(grads_dev, layer_ids, tile_row, tile_col).astype(jnp.float32)
    memory_tiles = take_tiles(memory_dev, layer_ids, tile_row, tile_col).astype(jnp.float32)
    combined = grad_tiles + memory_tiles
    return combined.reshape(combined.shape[0], TILE * TILE)


def selected_mask(layer_ids, block_ids, layers, tile_count):
    columns = layer_ids * (tile_count * tile_count) + block_ids
    all_columns = jnp.arange(layers * tile_count * tile_count, dtype=jnp.int32)
    chosen = jnp.any(columns[:, None] == all_columns[None, :], axis=0)
    return chosen.reshape(layers, tile_count, 1, tile_count, 1)


def filter_memory(grads_dev, memory_dev, chosen):
    layers, model_width, _ = grads_dev.shape
    tile_count = model_width // TILE
    accumulated = grads_dev.astype(jnp.float32) + memory_dev.astype(jnp.float32)
    shaped = accumulated.reshape(layers, tile_count, TILE, tile_count, TILE)
    filtered = jnp.where(chosen, jnp.float32(0.0), shaped).reshape(layers, model_width, model_width)
    mixed = (1.0 - filter_rate) * memory_dev.astype(jnp.float32) + filter_rate * filtered
    return mixed.astype(jnp.bfloat16)


def adam_rows(summed, weights_sel, first_old, second_old):
    first_sel = beta_one * first_old + (1.0 - beta_one) * summed
    second_sel = beta_two * second_old + (1.0 - beta_two) * summed * summed
    update = first_sel / (jnp.sqrt(second_sel) + adam_eps) + weight_decay * weights_sel
    return (first_sel, second_sel, update)


def layer_squares(member, values):
    return jnp.sum(member * jnp.sum(values * values, axis=1)[:, None], axis=0)


def trust_rows(member, weight_total, update_total):
    trust_ratio = jnp.sqrt(weight_total / (update_total + norm_eps))
    return jnp.sum(member * trust_ratio[None, :], axis=1)


def on_device(grads, memory, block_ids, layer_ids, master, first_moment, second_moment):
    layers, model_width, _ = grads.shape
    tile_count = model_width // TILE
    tile_row = block_ids // tile_count
    tile_col = block_ids % tile_count
    columns = layer_ids * (tile_count * tile_count) + block_ids
    member = (layer_ids[:, None] == jnp.arange(layers, dtype=jnp.int32)[None, :]).astype(
        jnp.float32
    )
    weights_sel = jnp.take(master, columns, axis=0)
    first_old = jnp.take(first_moment, columns, axis=0)
    second_old = jnp.take(second_moment, columns, axis=0)
    packed = pack_blocks(grads, memory, layer_ids, tile_row, tile_col)
    summed = lax.psum_scatter(packed, "dp", scatter_dimension=1, tiled=True)
    first_sel, second_sel, update = adam_rows(summed, weights_sel, first_old, second_old)
    weight_total, update_total = lax.psum(
        (layer_squares(member, weights_sel), layer_squares(member, update)), "dp"
    )
    scaled = trust_rows(member, weight_total, update_total)[:, None] * update
    step_blocks = lax.all_gather(scaled.astype(jnp.bfloat16), "dp", axis=1, tiled=True)
    new_memory = filter_memory(
        grads, memory, selected_mask(layer_ids, block_ids, layers, tile_count)
    )
    master_new = master.at[columns].set(weights_sel - learn_rate * scaled)
    first_new = first_moment.at[columns].set(first_sel)
    second_new = second_moment.at[columns].set(second_sel)
    return (new_memory, master_new, first_new, second_new, step_blocks)


def xor_bit(bit, flip):
    return bit if flip == 0 else 1 - bit


def pack_kernel(layers_smem, blocks_smem, grads_hbm, memory_hbm, master_ref, first_ref, second_ref,
                out_hbm, packed_ref, state_ref, member_ref,
                grads_ref, memory_ref, out_ref, grads_sem, memory_sem, out_sem):
    count = layers_smem.shape[0]
    layers = member_ref.shape[0]
    pieces = state_ref.shape[1] // count
    slabs = grads_ref.shape[0]
    tile_count = slabs // layers

    def moves(i):
        layer, rows = lax.div(i, tile_count), pl.ds(lax.rem(i, tile_count) * TILE, TILE)
        return (pltpu.make_async_copy(grads_hbm.at[layer, rows], grads_ref.at[i], grads_sem.at[i]),
                pltpu.make_async_copy(memory_hbm.at[layer, rows], memory_ref.at[i], memory_sem.at[i]),
                pltpu.make_async_copy(out_ref.at[i], out_hbm.at[layer, rows], out_sem.at[i]))

    @pl.loop(0, slabs)
    def _(i):
        moves(i)[0].start()
        moves(i)[1].start()

    for k in range(count):
        column = layers_smem[k] * (tile_count * tile_count) + blocks_smem[k]
        for s, ref in enumerate((master_ref, first_ref, second_ref)):
            line = ref[pl.ds(column, 1), :]
            for j in range(pieces):
                state_ref[s, j * count + k:j * count + k + 1, :] = line[:, j * TILE:(j + 1) * TILE]
        for l in range(layers):
            flag = jnp.where(layers_smem[k] == l, jnp.float32(1.0), jnp.float32(0.0))
            for j in range(pieces):
                member_ref[l, j * count + k:j * count + k + 1, :] = jnp.full((1, TILE), flag, jnp.float32)

    @pl.loop(0, slabs)
    def _(i):
        moves(i)[0].wait()
        moves(i)[1].wait()
        memory = memory_ref[i].astype(jnp.float32)
        total = grads_ref[i].astype(jnp.float32) + memory
        out_ref[i] = ((1.0 - filter_rate) * memory + filter_rate * total).astype(out_ref.dtype)
        for k in range(count):
            block = blocks_smem[k]

            @pl.when(layers_smem[k] * tile_count + lax.div(block, tile_count) == i)
            def _():
                lanes = pl.ds(pl.multiple_of(lax.rem(block, tile_count) * TILE, TILE), TILE)
                kept = memory_ref[i, :, lanes].astype(jnp.float32)
                packed_ref[pl.ds(k, TILE, stride=count), :] = grads_ref[i, :, lanes].astype(jnp.float32) + kept
                out_ref[i, :, lanes] = ((1.0 - filter_rate) * kept).astype(out_ref.dtype)

        moves(i)[2].start()

    @pl.loop(0, slabs)
    def _(i):
        moves(i)[2].wait()


def exchange_kernel(n, packed_ref, state_ref, member_ref, rows_ref, step_ref,
                    mine, recv1, send2, recv2, send3, recv3, stat_own, stat_in, stat_mid, stat_far,
                    s0, s1, r1, s2, r2, s3, r3, s4, r4, s5, r5, sz, sp, sc, rg):
    depth = n // 8
    layers = member_ref.shape[0]
    count = step_ref.shape[0]
    entries = step_ref.shape[1] // n
    pieces = entries // TILE
    me = lax.axis_index("dp")
    core = lax.rem(me, 2)
    x = lax.rem(lax.div(me, 2), 2)
    y = lax.rem(lax.div(me, 4), 2)
    z = lax.div(me, 8)

    def device(dz, dq, dc, back=False):
        far = lax.rem(z + (depth - dz if back else dz), depth) if dz else z
        return far * 8 + xor_bit(y, dq // 2) * 4 + xor_bit(x, dq % 2) * 2 + xor_bit(core, dc)

    def plane(dq):
        return xor_bit(y, dq // 2) * 2 + xor_bit(x, dq % 2)

    def copy(src, dst, send, recv, peer):
        return pltpu.make_async_remote_copy(
            src_ref=src, dst_ref=dst, send_sem=send, recv_sem=recv,
            device_id=(peer,), device_id_type=pl.DeviceIdType.MESH)

    barrier = pltpu.get_barrier_semaphore()
    peers = [device(0, i // 2, i % 2) for i in range(1, 8)] + [device(dz, 0, 0) for dz in range(1, depth)]
    for peer in peers:
        pl.semaphore_signal(barrier, inc=1, device_id=(peer,), device_id_type=pl.DeviceIdType.MESH)
    own_half = pltpu.make_async_copy(packed_ref.at[:, :, core], mine, s0.at[0])
    own_half.start()
    weights = state_ref[0]
    stat_own[...] = jnp.zeros_like(stat_own)
    for l in range(layers):
        stat_own[l:l + 1, :] = jnp.sum(member_ref[l] * (weights * weights), axis=0, keepdims=True)
    pl.semaphore_wait(barrier, len(peers))

    order = (3, 1, 2, 0)
    reach = sorted(range(1, depth), key=lambda dz: min(dz, depth - dz))
    targets = [(dz, lax.rem(z + dz, depth)) for dz in reach[::-1]] + [(0, z)]
    first_hop, second_hop, third_hop = {}, {}, {}
    for dz, at in targets:
        for dq in order:
            slot = dz * 4 + dq
            first_hop[slot] = copy(packed_ref.at[at, plane(dq), 1 - core], recv1.at[slot],
                                   s1.at[slot], r1.at[slot], device(0, 0, 1))
            first_hop[slot].start()
    own_half.wait()
    for dz, at in targets:
        for dq in order[:3]:
            slot, place = dz * 4 + dq, dz * 3 + dq - 1
            first_hop[slot].wait_recv()
            send2[place] = mine[at, plane(dq)] + recv1[slot]
            second_hop[place] = copy(send2.at[place], recv2.at[place], s2.at[place], r2.at[place], device(0, dq, 0))
            second_hop[place].start()
    here = plane(0)
    summed = None
    for dz, at in targets:
        first_hop[dz * 4].wait_recv()
        for dq in range(3):
            second_hop[dz * 3 + dq].wait_recv()
        part = (mine[at, here] + recv1[dz * 4]) + ((recv2[dz * 3] + recv2[dz * 3 + 1]) + recv2[dz * 3 + 2])
        if dz == 0:
            summed = part
        else:
            send3[dz - 1] = part
            third_hop[dz] = copy(send3.at[dz - 1], recv3.at[dz - 1], s3.at[dz - 1], r3.at[dz - 1], device(dz, 0, 0))
            third_hop[dz].start()
    for dz in range(1, depth):
        third_hop[dz].wait_recv()
        summed = summed + recv3[dz - 1]

    first_sel = beta_one * state_ref[1] + (1.0 - beta_one) * summed
    second_sel = beta_two * state_ref[2] + (1.0 - beta_two) * summed * summed
    update = first_sel / (jnp.sqrt(second_sel) + adam_eps) + weight_decay * weights
    rows_ref[1] = first_sel
    rows_ref[2] = second_sel
    for l in range(layers):
        stat_own[layers + l:layers + l + 1, :] = jnp.sum(member_ref[l] * (update * update), axis=0, keepdims=True)
    near = []
    for i in range(1, 8):
        hop = copy(stat_own, stat_in.at[i - 1], s4.at[i - 1], r4.at[i - 1], device(0, i // 2, i % 2))
        hop.start()
        near.append(hop)
    total = stat_own[...]
    for i in range(1, 8):
        near[i - 1].wait_recv()
        total = total + stat_in[i - 1]
    stat_mid[...] = total
    away = []
    for dz in range(1, depth):
        hop = copy(stat_mid, stat_far.at[dz - 1], s5.at[dz - 1], r5.at[dz - 1], device(dz, 0, 0))
        hop.start()
        away.append(hop)
    for dz in range(1, depth):
        away[dz - 1].wait_recv()
        total = total + stat_far[dz - 1]
    sums = jnp.sum(total, axis=1, keepdims=True)
    factor = jnp.zeros_like(update)
    for l in range(layers):
        ratio = jnp.sqrt(sums[l:l + 1] / (sums[layers + l:layers + l + 1] + norm_eps))
        factor = factor + member_ref[l] * ratio
    scaled = factor * update
    for j in range(pieces):
        lanes = pl.ds(pl.multiple_of(me * entries + j * TILE, TILE), TILE)
        step_ref[:, lanes] = scaled[j * count:(j + 1) * count].astype(step_ref.dtype)

    def chunk(dz, dq, dc):
        return step_ref.at[:, pl.ds(pl.multiple_of(device(dz, dq, dc, back=True) * entries, TILE), entries)]

    started = near + away + [hop for hops in (first_hop, second_hop, third_hop) for hop in hops.values()]

    def forward(dz, dq, dc, to_z, to_q, to_c, send, there):
        block = chunk(dz, dq, dc)
        hop = copy(block, block, send, rg.at[there], device(to_z, to_q, to_c))
        hop.start()
        started.append(hop)

    def arrived(dz, dq, dc):
        block = chunk(dz, dq, dc)
        at = (dz * 4 + dq) * 2 + dc
        copy(block, block, sz.at[0], rg.at[at], device(0, 0, 1)).wait_recv()

    def spread(dz):
        for dq in order[:3]:
            forward(dz, 0, 0, 0, dq, 0, sp.at[dz * 3 + dq - 1], (dz * 4 + dq) * 2)

    def hand_over(dz, dq):
        forward(dz, dq, 0, 0, 0, 1, sc.at[dz * 4 + dq], (dz * 4 + dq) * 2 + 1)

    for dz in range(1, depth):
        forward(0, 0, 0, dz, 0, 0, sz.at[dz - 1], dz * 8)
    spread(0)
    hand_over(0, 0)
    rows_ref[0] = weights - learn_rate * scaled
    for dz in reach:
        arrived(dz, 0, 0)
        spread(dz)
        hand_over(dz, 0)
    for dz in [0] + reach:
        for dq in (1, 2, 3):
            arrived(dz, dq, 0)
            hand_over(dz, dq)
    for dz in range(depth):
        for dq in range(4):
            arrived(dz, dq, 1)
    for hop in started:
        hop.wait_send()


def state_kernel(layers_smem, blocks_smem, rows_ref, step_ref, master_ref, first_ref, second_ref,
                 master_out, first_out, second_out, step_out, *, layer_rows):
    count = layers_smem.shape[0]
    pieces = rows_ref.shape[1] // count
    outs = ((master_ref, master_out), (first_ref, first_out), (second_ref, second_out))
    step_out[...] = step_ref[...]
    for old, new in outs:
        new[...] = old[...]
    for k in range(count):
        column = layers_smem[k] * layer_rows + blocks_smem[k]
        base = pl.ds(pl.multiple_of(lax.div(column, 8) * 8, 8), 8)
        hit = lax.broadcasted_iota(jnp.int32, (8, TILE), 0) == lax.rem(column, 8)
        for s, (_, new) in enumerate(outs):
            for j in range(pieces):
                lanes = slice(j * TILE, (j + 1) * TILE)
                line = rows_ref[s, j * count + k:j * count + k + 1, :]
                new[base, lanes] = jnp.where(hit, line, new[base, lanes])


def on_device_kernels(n, grads, memory, block_ids, layer_ids, master, first_moment, second_moment):
    layers, width, _ = grads.shape
    tile_count = width // TILE
    count = block_ids.shape[0]
    entries = master.shape[1]
    lines = entries // TILE * count
    depth = n // 8
    f32 = jnp.float32
    vmem, smem, hbm = (pl.BlockSpec(memory_space=m) for m in (pltpu.VMEM, pltpu.SMEM, pl.ANY))
    slabs = layers * tile_count
    dma = pltpu.SemaphoreType.DMA
    new_memory, packed, state, member = pl.pallas_call(
        pack_kernel,
        in_specs=[smem, smem, hbm, hbm] + [vmem] * 3,
        out_specs=[hbm] + [vmem] * 3,
        out_shape=[
            jax.ShapeDtypeStruct(memory.shape, jnp.bfloat16),
            jax.ShapeDtypeStruct((n * lines, TILE), f32),
            jax.ShapeDtypeStruct((3, lines, TILE), f32),
            jax.ShapeDtypeStruct((layers, lines, TILE), f32)],
        scratch_shapes=[pltpu.VMEM((slabs, TILE, width), jnp.bfloat16)] * 3 + [dma((slabs,))] * 3,
        name="pack",
    )(layer_ids, block_ids, grads, memory, master, first_moment, second_moment)
    stat_rows = -(-2 * layers // 8) * 8
    rows, gathered = pl.pallas_call(
        functools.partial(exchange_kernel, n),
        out_shape=[jax.ShapeDtypeStruct((3, lines, TILE), f32),
                   jax.ShapeDtypeStruct((count, n * entries), jnp.bfloat16)],
        in_specs=[hbm, vmem, vmem],
        out_specs=[vmem] * 2,
        scratch_shapes=[
            pltpu.VMEM((depth, 4, lines, TILE), f32),
            pltpu.VMEM((depth * 4, lines, TILE), f32),
            pltpu.VMEM((depth * 3, lines, TILE), f32),
            pltpu.VMEM((depth * 3, lines, TILE), f32),
            pltpu.VMEM((depth - 1, lines, TILE), f32),
            pltpu.VMEM((depth - 1, lines, TILE), f32),
            pltpu.VMEM((stat_rows, TILE), f32),
            pltpu.VMEM((7, stat_rows, TILE), f32),
            pltpu.VMEM((stat_rows, TILE), f32),
            pltpu.VMEM((depth - 1, stat_rows, TILE), f32),
            dma((1,)), dma((depth * 4,)), dma((depth * 4,)), dma((depth * 3,)), dma((depth * 3,)), dma((depth - 1,)), dma((depth - 1,)),
            dma((7,)), dma((7,)), dma((depth - 1,)), dma((depth - 1,)),
            dma((depth - 1,)), dma((depth * 3,)), dma((depth * 4,)), dma((n,))],
        compiler_params=pltpu.CompilerParams(collective_id=0, has_side_effects=True),
        name="exchange",
    )(packed.reshape(depth, 4, 2, lines, TILE), state, member)
    like = jax.ShapeDtypeStruct(master.shape, f32)
    master_new, first_new, second_new, step_blocks = pl.pallas_call(
        functools.partial(state_kernel, layer_rows=tile_count * tile_count),
        out_shape=[like] * 3 + [jax.ShapeDtypeStruct(gathered.shape, jnp.bfloat16)],
        in_specs=[smem, smem] + [vmem] * 5,
        out_specs=[vmem] * 4,
        name="state",
    )(layer_ids, block_ids, rows, gathered, master, first_moment, second_moment)
    return (new_memory, master_new, first_new, second_new, step_blocks)


def solution(mesh):
    n = mesh.shape["dp"]

    def body(*args):
        entries, count = args[4].shape[1], args[2].shape[0]
        if n % 8 == 0 and n > 8 and entries % TILE == 0 and count % 16 == 0:
            return on_device_kernels(n, *args)
        return on_device(*args)

    in_specs = (
        P("dp", None, None),
        P("dp", None, None),
        P(),
        P(),
        P(None, "dp"),
        P(None, "dp"),
        P(None, "dp"),
    )
    out_specs = (P("dp", None, None), P(None, "dp"), P(None, "dp"), P(None, "dp"), P())
    return jax.shard_map(
        body, mesh=mesh, in_specs=in_specs, out_specs=out_specs, check_vma=False
    )
```

```python
import functools

import jax
import jax.numpy as jnp
from jax import lax
from jax.experimental import pallas as pl
from jax.experimental.pallas import tpu as pltpu
from jax.sharding import PartitionSpec as P

TILE = 128


filter_rate = 0.3
beta_one = 0.9
beta_two = 0.999
adam_eps = 1e-06
weight_decay = 0.01
learn_rate = 0.01
norm_eps = 1e-06


def take_tiles(source, layer_ids, tile_row, tile_col):

    def single(layer_id, row_tile, col_tile):
        return lax.dynamic_slice(
            source, (layer_id, row_tile * TILE, col_tile * TILE), (1, TILE, TILE)
        )[0]

    return jax.vmap(single)(layer_ids, tile_row, tile_col)


def pack_blocks(grads_dev, memory_dev, layer_ids, tile_row, tile_col):
    grad_tiles = take_tiles(grads_dev, layer_ids, tile_row, tile_col).astype(jnp.float32)
    memory_tiles = take_tiles(memory_dev, layer_ids, tile_row, tile_col).astype(jnp.float32)
    combined = grad_tiles + memory_tiles
    return combined.reshape(combined.shape[0], TILE * TILE)


def selected_mask(layer_ids, block_ids, layers, tile_count):
    columns = layer_ids * (tile_count * tile_count) + block_ids
    all_columns = jnp.arange(layers * tile_count * tile_count, dtype=jnp.int32)
    chosen = jnp.any(columns[:, None] == all_columns[None, :], axis=0)
    return chosen.reshape(layers, tile_count, 1, tile_count, 1)


def filter_memory(grads_dev, memory_dev, chosen):
    layers, model_width, _ = grads_dev.shape
    tile_count = model_width // TILE
    accumulated = grads_dev.astype(jnp.float32) + memory_dev.astype(jnp.float32)
    shaped = accumulated.reshape(layers, tile_count, TILE, tile_count, TILE)
    filtered = jnp.where(chosen, jnp.float32(0.0), shaped).reshape(layers, model_width, model_width)
    mixed = (1.0 - filter_rate) * memory_dev.astype(jnp.float32) + filter_rate * filtered
    return mixed.astype(jnp.bfloat16)


def adam_rows(summed, weights_sel, first_old, second_old):
    first_sel = beta_one * first_old + (1.0 - beta_one) * summed
    second_sel = beta_two * second_old + (1.0 - beta_two) * summed * summed
    update = first_sel / (jnp.sqrt(second_sel) + adam_eps) + weight_decay * weights_sel
    return (first_sel, second_sel, update)


def layer_squares(member, values):
    return jnp.sum(member * jnp.sum(values * values, axis=1)[:, None], axis=0)


def trust_rows(member, weight_total, update_total):
    trust_ratio = jnp.sqrt(weight_total / (update_total + norm_eps))
    return jnp.sum(member * trust_ratio[None, :], axis=1)


def on_device(grads, memory, block_ids, layer_ids, master, first_moment, second_moment):
    layers, model_width, _ = grads.shape
    tile_count = model_width // TILE
    tile_row = block_ids // tile_count
    tile_col = block_ids % tile_count
    columns = layer_ids * (tile_count * tile_count) + block_ids
    member = (layer_ids[:, None] == jnp.arange(layers, dtype=jnp.int32)[None, :]).astype(
        jnp.float32
    )
    weights_sel = jnp.take(master, columns, axis=0)
    first_old = jnp.take(first_moment, columns, axis=0)
    second_old = jnp.take(second_moment, columns, axis=0)
    packed = pack_blocks(grads, memory, layer_ids, tile_row, tile_col)
    summed = lax.psum_scatter(packed, "dp", scatter_dimension=1, tiled=True)
    first_sel, second_sel, update = adam_rows(summed, weights_sel, first_old, second_old)
    weight_total, update_total = lax.psum(
        (layer_squares(member, weights_sel), layer_squares(member, update)), "dp"
    )
    scaled = trust_rows(member, weight_total, update_total)[:, None] * update
    step_blocks = lax.all_gather(scaled.astype(jnp.bfloat16), "dp", axis=1, tiled=True)
    new_memory = filter_memory(
        grads, memory, selected_mask(layer_ids, block_ids, layers, tile_count)
    )
    master_new = master.at[columns].set(weights_sel - learn_rate * scaled)
    first_new = first_moment.at[columns].set(first_sel)
    second_new = second_moment.at[columns].set(second_sel)
    return (new_memory, master_new, first_new, second_new, step_blocks)


def xor_bit(bit, flip):
    return bit if flip == 0 else 1 - bit


def pack_kernel(layers_smem, blocks_smem, grads_hbm, memory_hbm, master_hbm, first_hbm, second_hbm,
                out_hbm, packed_hbm, state_ref, member_ref,
                grads_ref, memory_ref, out_ref, grad_tiles, memory_tiles, packed_ref, old_ref, rate_ref,
                grads_sem, memory_sem, out_sem, tile_sem, old_sem, packed_sem):
    count = layers_smem.shape[0]
    layers = member_ref.shape[0]
    pieces = state_ref.shape[1] // count
    slabs = grads_ref.shape[0]
    tile_count = slabs // layers

    def moves(i):
        layer, rows = lax.div(i, tile_count), pl.ds(pl.multiple_of(lax.rem(i, tile_count) * TILE, TILE), TILE)
        return ((grads_hbm.at[layer, rows], grads_ref.at[i], grads_sem.at[i]),
                (memory_hbm.at[layer, rows], memory_ref.at[i], memory_sem.at[i]),
                (out_ref.at[i], out_hbm.at[layer, rows], out_sem.at[i]))

    tiles = []
    for k in range(count):
        block = blocks_smem[k]
        rows = pl.ds(pl.multiple_of(lax.div(block, tile_count) * TILE, TILE), TILE)
        lanes = pl.ds(pl.multiple_of(lax.rem(block, tile_count) * TILE, TILE), TILE)
        for s, (source, held) in enumerate(((grads_hbm, grad_tiles), (memory_hbm, memory_tiles))):
            tiles.append(pltpu.make_async_copy(
                source.at[layers_smem[k], rows, lanes], held.at[k], tile_sem.at[s * count + k]))
            tiles[-1].start()

    @pl.loop(0, slabs)
    def _(i):
        grads_in, memory_in, _ = moves(i)
        pltpu.make_async_copy(*grads_in).start()
        pltpu.make_async_copy(*memory_in).start()

    olds = []
    for s, source in enumerate((master_hbm, first_hbm, second_hbm)):
        olds.append(pltpu.make_async_copy(source, old_ref.at[s], old_sem.at[s]))
        olds[-1].start()

    @pl.loop(0, slabs)
    def _(i):
        for t in range(tile_count):
            rate_ref[i * tile_count + t] = jnp.float32(filter_rate)

    for k in range(count):
        rate_ref[layers_smem[k] * (tile_count * tile_count) + blocks_smem[k]] = jnp.float32(0.0)
    for k in range(count):
        tiles[2 * k].wait()
        tiles[2 * k + 1].wait()
        packed_ref[pl.ds(k, TILE, stride=count), :] = (
            grad_tiles[k].astype(jnp.float32) + memory_tiles[k].astype(jnp.float32))
    packed_out = pltpu.make_async_copy(packed_ref, packed_hbm, packed_sem.at[0])
    packed_out.start()

    @pl.loop(0, slabs)
    def _(i):
        grads_in, memory_in, out = moves(i)
        pltpu.make_async_copy(*grads_in).wait()
        pltpu.make_async_copy(*memory_in).wait()
        for t in range(tile_count):
            lanes = slice(t * TILE, (t + 1) * TILE)
            memory = memory_ref[i, :, lanes].astype(jnp.float32)
            total = grads_ref[i, :, lanes].astype(jnp.float32) + memory
            mixed = (1.0 - filter_rate) * memory + rate_ref[i * tile_count + t] * total
            out_ref[i, :, lanes] = mixed.astype(out_ref.dtype)
        pltpu.make_async_copy(*out).start()

    for old in olds:
        old.wait()
    for k in range(count):
        column = layers_smem[k] * (tile_count * tile_count) + blocks_smem[k]
        for s in range(3):
            line = old_ref[s, pl.ds(column, 1), :]
            for j in range(pieces):
                state_ref[s, j * count + k:j * count + k + 1, :] = line[:, j * TILE:(j + 1) * TILE]
        for l in range(layers):
            flag = jnp.where(layers_smem[k] == l, jnp.float32(1.0), jnp.float32(0.0))
            for j in range(pieces):
                member_ref[l, j * count + k:j * count + k + 1, :] = jnp.full((1, TILE), flag, jnp.float32)
    packed_out.wait()

    @pl.loop(0, slabs)
    def _(i):
        pltpu.make_async_copy(*moves(i)[2]).wait()


def exchange_kernel(n, packed_ref, state_ref, member_ref, rows_ref, step_ref,
                    mine, recv1, send2, recv2, send3, recv3, stat_own, stat_in, stat_mid, stat_far, update_own, update_far,
                    s0, s1, r1, s2, r2, s3, r3, s4, r4, s5, r5, sz, rz, sp, sc, rg):
    depth = n // 8
    layers = member_ref.shape[0]
    count = step_ref.shape[0]
    entries = step_ref.shape[1] // n
    pieces = entries // TILE
    me = lax.axis_index("dp")
    core = lax.rem(me, 2)
    x = lax.rem(lax.div(me, 2), 2)
    y = lax.rem(lax.div(me, 4), 2)
    z = lax.div(me, 8)

    def device(dz, dq, dc, back=False):
        far = lax.rem(z + (depth - dz if back else dz), depth) if dz else z
        return far * 8 + xor_bit(y, dq // 2) * 4 + xor_bit(x, dq % 2) * 2 + xor_bit(core, dc)

    def plane(dq):
        return xor_bit(y, dq // 2) * 2 + xor_bit(x, dq % 2)

    def copy(src, dst, send, recv, peer):
        return pltpu.make_async_remote_copy(
            src_ref=src, dst_ref=dst, send_sem=send, recv_sem=recv,
            device_id=(peer,), device_id_type=pl.DeviceIdType.MESH)

    barrier = pltpu.get_barrier_semaphore()
    peers = [device(0, i // 2, i % 2) for i in range(1, 8)] + [device(dz, 0, 0) for dz in range(1, depth)]
    for peer in peers:
        pl.semaphore_signal(barrier, inc=1, device_id=(peer,), device_id_type=pl.DeviceIdType.MESH)
    own_half = pltpu.make_async_copy(packed_ref.at[:, :, core], mine, s0.at[0])
    own_half.start()
    weights = state_ref[0]
    stat_own[...] = jnp.zeros_like(stat_own)
    for l in range(layers):
        stat_own[l:l + 1, :] = jnp.sum(member_ref[l] * (weights * weights), axis=0, keepdims=True)
    pl.semaphore_wait(barrier, len(peers))

    order = (3, 1, 2, 0)
    reach = sorted(range(1, depth), key=lambda dz: min(dz, depth - dz))
    targets = [(dz, lax.rem(z + dz, depth)) for dz in reach[::-1]] + [(0, z)]
    first_hop, second_hop, third_hop = {}, {}, {}
    for dz, at in targets:
        for dq in order:
            slot = dz * 4 + dq
            first_hop[slot] = copy(packed_ref.at[at, plane(dq), 1 - core], recv1.at[slot],
                                   s1.at[slot], r1.at[slot], device(0, 0, 1))
            first_hop[slot].start()
    own_half.wait()
    for dz, at in targets:
        for dq in order[:3]:
            slot, place = dz * 4 + dq, dz * 3 + dq - 1
            first_hop[slot].wait_recv()
            send2[place] = mine[at, plane(dq)] + recv1[slot]
            second_hop[place] = copy(send2.at[place], recv2.at[place], s2.at[place], r2.at[place], device(0, dq, 0))
            second_hop[place].start()
    here = plane(0)
    summed = None
    for dz, at in targets:
        first_hop[dz * 4].wait_recv()
        for dq in range(3):
            second_hop[dz * 3 + dq].wait_recv()
        part = (mine[at, here] + recv1[dz * 4]) + ((recv2[dz * 3] + recv2[dz * 3 + 1]) + recv2[dz * 3 + 2])
        if dz == 0:
            summed = part
        else:
            send3[dz - 1] = part
            third_hop[dz] = copy(send3.at[dz - 1], recv3.at[dz - 1], s3.at[dz - 1], r3.at[dz - 1], device(dz, 0, 0))
            third_hop[dz].start()
    for dz in range(1, depth):
        third_hop[dz].wait_recv()
        summed = summed + recv3[dz - 1]

    first_sel = beta_one * state_ref[1] + (1.0 - beta_one) * summed
    second_sel = beta_two * state_ref[2] + (1.0 - beta_two) * summed * summed
    update = first_sel / (jnp.sqrt(second_sel) + adam_eps) + weight_decay * weights
    rows_ref[1] = first_sel
    rows_ref[2] = second_sel
    for l in range(layers):
        stat_own[layers + l:layers + l + 1, :] = jnp.sum(member_ref[l] * (update * update), axis=0, keepdims=True)
    def spot(dq, dc):
        return plane(dq) * 2 + xor_bit(core, dc)

    near, away, ahead = [], [], {}
    for i in range(1, 8):
        near.append(copy(stat_own, stat_in.at[spot(0, 0)], s4.at[i - 1], r4.at[i - 1], device(0, i // 2, i % 2)))
        near[-1].start()
    update_own[...] = update
    for dz in range(1, depth):
        ahead[dz] = copy(update_own, update_far.at[dz - 1], sz.at[dz - 1], rz.at[dz - 1], device(dz, 0, 0))
        ahead[dz].start()
    stat_in[spot(0, 0)] = stat_own[...]
    for i in range(1, 8):
        slot = stat_in.at[spot(i // 2, i % 2)]
        copy(stat_own, slot, s4.at[i - 1], r4.at[i - 1], device(0, i // 2, i % 2)).wait_recv()
    total = stat_in[0]
    for i in range(1, 8):
        total = total + stat_in[i]
    stat_mid[...] = total
    for dz in range(1, depth):
        away.append(copy(stat_mid, stat_far.at[z], s5.at[dz - 1], r5.at[dz - 1], device(dz, 0, 0)))
        away[-1].start()
    stat_far[z] = total
    for dz in range(1, depth):
        slot = stat_far.at[lax.rem(z + depth - dz, depth)]
        copy(stat_mid, slot, s5.at[dz - 1], r5.at[dz - 1], device(dz, 0, 0)).wait_recv()
    total = stat_far[0]
    for at in range(1, depth):
        total = total + stat_far[at]
    sums = jnp.sum(total, axis=1, keepdims=True)
    factor = jnp.zeros_like(update)
    for l in range(layers):
        ratio = jnp.sqrt(sums[l:l + 1] / (sums[layers + l:layers + l + 1] + norm_eps))
        factor = factor + member_ref[l] * ratio

    def place(dz, scaled):
        owner = device(dz, 0, 0, back=True)
        for j in range(pieces):
            lanes = pl.ds(pl.multiple_of(owner * entries + j * TILE, TILE), TILE)
            step_ref[:, lanes] = scaled[j * count:(j + 1) * count].astype(step_ref.dtype)

    def chunk(dz, dq, dc):
        return step_ref.at[:, pl.ds(pl.multiple_of(device(dz, dq, dc, back=True) * entries, TILE), entries)]

    started = near + away + list(ahead.values()) + [hop for hops in (first_hop, second_hop, third_hop) for hop in hops.values()]

    def forward(dz, dq, dc, to_z, to_q, to_c, send, there):
        block = chunk(dz, dq, dc)
        hop = copy(block, block, send, rg.at[there], device(to_z, to_q, to_c))
        hop.start()
        started.append(hop)

    def arrived(dz, dq, dc):
        block = chunk(dz, dq, dc)
        at = (dz * 4 + dq) * 2 + dc
        copy(block, block, sc.at[0], rg.at[at], device(0, 0, 1)).wait_recv()

    def spread(dz):
        for dq in order[:3]:
            forward(dz, 0, 0, 0, dq, 0, sp.at[dz * 3 + dq - 1], (dz * 4 + dq) * 2)

    def hand_over(dz, dq):
        forward(dz, dq, 0, 0, 0, 1, sc.at[dz * 4 + dq], (dz * 4 + dq) * 2 + 1)

    scaled = factor * update
    place(0, scaled)
    spread(0)
    hand_over(0, 0)
    for dz in reach:
        ahead[dz].wait_recv()
        place(dz, factor * update_far[dz - 1])
        spread(dz)
        hand_over(dz, 0)
    rows_ref[0] = weights - learn_rate * scaled
    for dz in [0] + reach:
        for dq in (1, 2, 3):
            arrived(dz, dq, 0)
            hand_over(dz, dq)
    for dz in range(depth):
        for dq in range(4):
            arrived(dz, dq, 1)
    for hop in started:
        hop.wait_send()


def state_kernel(layers_smem, blocks_smem, rows_ref, step_ref, master_ref, first_ref, second_ref,
                 master_out, first_out, second_out, step_out, *, layer_rows):
    count = layers_smem.shape[0]
    pieces = rows_ref.shape[1] // count
    outs = ((master_ref, master_out), (first_ref, first_out), (second_ref, second_out))
    step_out[...] = step_ref[...]
    for old, new in outs:
        new[...] = old[...]
    for k in range(count):
        column = layers_smem[k] * layer_rows + blocks_smem[k]
        base = pl.ds(pl.multiple_of(lax.div(column, 8) * 8, 8), 8)
        hit = lax.broadcasted_iota(jnp.int32, (8, TILE), 0) == lax.rem(column, 8)
        for s, (_, new) in enumerate(outs):
            for j in range(pieces):
                lanes = slice(j * TILE, (j + 1) * TILE)
                line = rows_ref[s, j * count + k:j * count + k + 1, :]
                new[base, lanes] = jnp.where(hit, line, new[base, lanes])


def on_device_kernels(n, grads, memory, block_ids, layer_ids, master, first_moment, second_moment):
    layers, width, _ = grads.shape
    tile_count = width // TILE
    count = block_ids.shape[0]
    entries = master.shape[1]
    lines = entries // TILE * count
    depth = n // 8
    f32 = jnp.float32
    vmem, smem, hbm = (pl.BlockSpec(memory_space=m) for m in (pltpu.VMEM, pltpu.SMEM, pl.ANY))
    slabs = layers * tile_count
    dma = pltpu.SemaphoreType.DMA
    new_memory, packed, state, member = pl.pallas_call(
        pack_kernel,
        in_specs=[smem, smem] + [hbm] * 5,
        out_specs=[hbm] * 2 + [vmem] * 2,
        out_shape=[
            jax.ShapeDtypeStruct(memory.shape, jnp.bfloat16),
            jax.ShapeDtypeStruct((n * lines, TILE), f32),
            jax.ShapeDtypeStruct((3, lines, TILE), f32),
            jax.ShapeDtypeStruct((layers, lines, TILE), f32)],
        scratch_shapes=[pltpu.VMEM((slabs, TILE, width), jnp.bfloat16)] * 3 + [
            pltpu.VMEM((count, TILE, TILE), jnp.bfloat16),
            pltpu.VMEM((count, TILE, TILE), jnp.bfloat16),
            pltpu.VMEM((n * lines, TILE), f32),
            pltpu.VMEM((3,) + master.shape, f32),
            pltpu.SMEM((slabs * tile_count,), f32),
            dma((slabs,)), dma((slabs,)), dma((slabs,)), dma((2 * count,)), dma((3,)), dma((1,))],
        name="pack",
    )(layer_ids, block_ids, grads, memory, master, first_moment, second_moment)
    stat_rows = -(-2 * layers // 8) * 8
    rows, gathered = pl.pallas_call(
        functools.partial(exchange_kernel, n),
        out_shape=[jax.ShapeDtypeStruct((3, lines, TILE), f32),
                   jax.ShapeDtypeStruct((count, n * entries), jnp.bfloat16)],
        in_specs=[hbm, vmem, vmem],
        out_specs=[vmem] * 2,
        scratch_shapes=[
            pltpu.VMEM((depth, 4, lines, TILE), f32),
            pltpu.VMEM((depth * 4, lines, TILE), f32),
            pltpu.VMEM((depth * 3, lines, TILE), f32),
            pltpu.VMEM((depth * 3, lines, TILE), f32),
            pltpu.VMEM((depth - 1, lines, TILE), f32),
            pltpu.VMEM((depth - 1, lines, TILE), f32),
            pltpu.VMEM((stat_rows, TILE), f32),
            pltpu.VMEM((8, stat_rows, TILE), f32),
            pltpu.VMEM((stat_rows, TILE), f32),
            pltpu.VMEM((depth, stat_rows, TILE), f32),
            pltpu.VMEM((lines, TILE), f32),
            pltpu.VMEM((depth - 1, lines, TILE), f32),
            dma((1,)), dma((depth * 4,)), dma((depth * 4,)), dma((depth * 3,)), dma((depth * 3,)), dma((depth - 1,)), dma((depth - 1,)),
            dma((7,)), dma((7,)), dma((depth - 1,)), dma((depth - 1,)),
            dma((depth - 1,)), dma((depth - 1,)), dma((depth * 3,)), dma((depth * 4,)), dma((n,))],
        compiler_params=pltpu.CompilerParams(collective_id=0, has_side_effects=True),
        name="exchange",
    )(packed.reshape(depth, 4, 2, lines, TILE), state, member)
    like = jax.ShapeDtypeStruct(master.shape, f32)
    master_new, first_new, second_new, step_blocks = pl.pallas_call(
        functools.partial(state_kernel, layer_rows=tile_count * tile_count),
        out_shape=[like] * 3 + [jax.ShapeDtypeStruct(gathered.shape, jnp.bfloat16)],
        in_specs=[smem, smem] + [vmem] * 5,
        out_specs=[vmem] * 4,
        name="state",
    )(layer_ids, block_ids, rows, gathered, master, first_moment, second_moment)
    return (new_memory, master_new, first_new, second_new, step_blocks)


def solution(mesh):
    n = mesh.shape["dp"]

    def body(*args):
        entries, count = args[4].shape[1], args[2].shape[0]
        if n % 8 == 0 and n > 8 and entries % TILE == 0 and count % 16 == 0:
            return on_device_kernels(n, *args)
        return on_device(*args)

    in_specs = (
        P("dp", None, None),
        P("dp", None, None),
        P(),
        P(),
        P(None, "dp"),
        P(None, "dp"),
        P(None, "dp"),
    )
    out_specs = (P("dp", None, None), P(None, "dp"), P(None, "dp"), P(None, "dp"), P())
    return jax.shard_map(
        body, mesh=mesh, in_specs=in_specs, out_specs=out_specs, check_vma=False
    )
```

```python
import functools

import jax
import jax.numpy as jnp
from jax import lax
from jax.experimental import pallas as pl
from jax.experimental.pallas import tpu as pltpu
from jax.sharding import PartitionSpec as P

TILE = 128


filter_rate = 0.3
beta_one = 0.9
beta_two = 0.999
adam_eps = 1e-06
weight_decay = 0.01
learn_rate = 0.01
norm_eps = 1e-06


def take_tiles(source, layer_ids, tile_row, tile_col):

    def single(layer_id, row_tile, col_tile):
        return lax.dynamic_slice(
            source, (layer_id, row_tile * TILE, col_tile * TILE), (1, TILE, TILE)
        )[0]

    return jax.vmap(single)(layer_ids, tile_row, tile_col)


def pack_blocks(grads_dev, memory_dev, layer_ids, tile_row, tile_col):
    grad_tiles = take_tiles(grads_dev, layer_ids, tile_row, tile_col).astype(jnp.float32)
    memory_tiles = take_tiles(memory_dev, layer_ids, tile_row, tile_col).astype(jnp.float32)
    combined = grad_tiles + memory_tiles
    return combined.reshape(combined.shape[0], TILE * TILE)


def selected_mask(layer_ids, block_ids, layers, tile_count):
    columns = layer_ids * (tile_count * tile_count) + block_ids
    all_columns = jnp.arange(layers * tile_count * tile_count, dtype=jnp.int32)
    chosen = jnp.any(columns[:, None] == all_columns[None, :], axis=0)
    return chosen.reshape(layers, tile_count, 1, tile_count, 1)


def filter_memory(grads_dev, memory_dev, chosen):
    layers, model_width, _ = grads_dev.shape
    tile_count = model_width // TILE
    accumulated = grads_dev.astype(jnp.float32) + memory_dev.astype(jnp.float32)
    shaped = accumulated.reshape(layers, tile_count, TILE, tile_count, TILE)
    filtered = jnp.where(chosen, jnp.float32(0.0), shaped).reshape(layers, model_width, model_width)
    mixed = (1.0 - filter_rate) * memory_dev.astype(jnp.float32) + filter_rate * filtered
    return mixed.astype(jnp.bfloat16)


def adam_rows(summed, weights_sel, first_old, second_old):
    first_sel = beta_one * first_old + (1.0 - beta_one) * summed
    second_sel = beta_two * second_old + (1.0 - beta_two) * summed * summed
    update = first_sel / (jnp.sqrt(second_sel) + adam_eps) + weight_decay * weights_sel
    return (first_sel, second_sel, update)


def layer_squares(member, values):
    return jnp.sum(member * jnp.sum(values * values, axis=1)[:, None], axis=0)


def trust_rows(member, weight_total, update_total):
    trust_ratio = jnp.sqrt(weight_total / (update_total + norm_eps))
    return jnp.sum(member * trust_ratio[None, :], axis=1)


def on_device(grads, memory, block_ids, layer_ids, master, first_moment, second_moment):
    layers, model_width, _ = grads.shape
    tile_count = model_width // TILE
    tile_row = block_ids // tile_count
    tile_col = block_ids % tile_count
    columns = layer_ids * (tile_count * tile_count) + block_ids
    member = (layer_ids[:, None] == jnp.arange(layers, dtype=jnp.int32)[None, :]).astype(
        jnp.float32
    )
    weights_sel = jnp.take(master, columns, axis=0)
    first_old = jnp.take(first_moment, columns, axis=0)
    second_old = jnp.take(second_moment, columns, axis=0)
    packed = pack_blocks(grads, memory, layer_ids, tile_row, tile_col)
    summed = lax.psum_scatter(packed, "dp", scatter_dimension=1, tiled=True)
    first_sel, second_sel, update = adam_rows(summed, weights_sel, first_old, second_old)
    weight_total, update_total = lax.psum(
        (layer_squares(member, weights_sel), layer_squares(member, update)), "dp"
    )
    scaled = trust_rows(member, weight_total, update_total)[:, None] * update
    step_blocks = lax.all_gather(scaled.astype(jnp.bfloat16), "dp", axis=1, tiled=True)
    new_memory = filter_memory(
        grads, memory, selected_mask(layer_ids, block_ids, layers, tile_count)
    )
    master_new = master.at[columns].set(weights_sel - learn_rate * scaled)
    first_new = first_moment.at[columns].set(first_sel)
    second_new = second_moment.at[columns].set(second_sel)
    return (new_memory, master_new, first_new, second_new, step_blocks)


def xor_bit(bit, flip):
    return bit if flip == 0 else 1 - bit


def pack_kernel(layers_smem, blocks_smem, grads_hbm, memory_hbm, master_hbm, first_hbm, second_hbm,
                packed_hbm, state_ref, member_ref, rate_ref,
                grad_tiles, memory_tiles, packed_ref, old_ref, tile_sem, old_sem, packed_sem):
    count = layers_smem.shape[0]
    layers = member_ref.shape[0]
    pieces = state_ref.shape[1] // count
    blocks = rate_ref.shape[0]
    layer_tiles = blocks // layers
    tile_count = grads_hbm.shape[1] // TILE

    tiles = []
    for k in range(count):
        block = blocks_smem[k]
        rows = pl.ds(pl.multiple_of(lax.div(block, tile_count) * TILE, TILE), TILE)
        lanes = pl.ds(pl.multiple_of(lax.rem(block, tile_count) * TILE, TILE), TILE)
        for s, (source, held) in enumerate(((grads_hbm, grad_tiles), (memory_hbm, memory_tiles))):
            tiles.append(pltpu.make_async_copy(
                source.at[layers_smem[k], rows, lanes], held.at[k], tile_sem.at[s * count + k]))
            tiles[-1].start()
    olds = []
    for s, source in enumerate((master_hbm, first_hbm, second_hbm)):
        olds.append(pltpu.make_async_copy(source, old_ref.at[s], old_sem.at[s]))
        olds[-1].start()

    for t in range(blocks):
        rate_ref[t] = jnp.float32(filter_rate)
    for k in range(count):
        rate_ref[layers_smem[k] * layer_tiles + blocks_smem[k]] = jnp.float32(0.0)
        for l in range(layers):
            flag = jnp.where(layers_smem[k] == l, jnp.float32(1.0), jnp.float32(0.0))
            for j in range(pieces):
                member_ref[l, j * count + k:j * count + k + 1, :] = jnp.full((1, TILE), flag, jnp.float32)
    for k in range(count):
        tiles[2 * k].wait()
        tiles[2 * k + 1].wait()
        packed_ref[pl.ds(k, TILE, stride=count), :] = (
            grad_tiles[k].astype(jnp.float32) + memory_tiles[k].astype(jnp.float32))
    packed_out = pltpu.make_async_copy(packed_ref, packed_hbm, packed_sem.at[0])
    packed_out.start()
    for old in olds:
        old.wait()
    for k in range(count):
        column = layers_smem[k] * layer_tiles + blocks_smem[k]
        for s in range(3):
            line = old_ref[s, pl.ds(column, 1), :]
            for j in range(pieces):
                state_ref[s, j * count + k:j * count + k + 1, :] = line[:, j * TILE:(j + 1) * TILE]
    packed_out.wait()


def exchange_kernel(n, packed_ref, state_ref, member_ref, rate_ref, grads_hbm, memory_hbm, rows_ref, step_ref, out_hbm,
                    mine, recv1, send2, recv2, send3, recv3, stat_own, stat_in, stat_mid, stat_far, updates, grads_ref, memory_ref, out_ref,
                    s0, s1, r1, s2, r2, s3, r3, s4, r4, s5, r5, sz, sp, ru, sc, rg,
                    grads_sem, memory_sem, out_sem):
    depth = n // 8
    layers = member_ref.shape[0]
    count = step_ref.shape[0]
    entries = step_ref.shape[1] // n
    pieces = entries // TILE
    me = lax.axis_index("dp")
    core = lax.rem(me, 2)
    x = lax.rem(lax.div(me, 2), 2)
    y = lax.rem(lax.div(me, 4), 2)
    z = lax.div(me, 8)

    def device(dz, dq, dc, back=False):
        far = lax.rem(z + (depth - dz if back else dz), depth) if dz else z
        return far * 8 + xor_bit(y, dq // 2) * 4 + xor_bit(x, dq % 2) * 2 + xor_bit(core, dc)

    def plane(dq):
        return xor_bit(y, dq // 2) * 2 + xor_bit(x, dq % 2)

    def copy(src, dst, send, recv, peer):
        return pltpu.make_async_remote_copy(
            src_ref=src, dst_ref=dst, send_sem=send, recv_sem=recv,
            device_id=(peer,), device_id_type=pl.DeviceIdType.MESH)

    barrier = pltpu.get_barrier_semaphore()
    peers = [device(0, i // 2, i % 2) for i in range(1, 8)] + [device(dz, 0, 0) for dz in range(1, depth)]
    for peer in peers:
        pl.semaphore_signal(barrier, inc=1, device_id=(peer,), device_id_type=pl.DeviceIdType.MESH)
    slabs = grads_ref.shape[0]
    tile_count = slabs // layers

    def moves(i):
        layer, rows = lax.div(i, tile_count), pl.ds(pl.multiple_of(lax.rem(i, tile_count) * TILE, TILE), TILE)
        return ((grads_hbm.at[layer, rows], grads_ref.at[i], grads_sem.at[i]),
                (memory_hbm.at[layer, rows], memory_ref.at[i], memory_sem.at[i]),
                (out_ref.at[i], out_hbm.at[layer, rows], out_sem.at[i]))

    def filter_slabs(start, stop):
        @pl.loop(start, stop)
        def _(i):
            grads_in, memory_in, out = moves(i)
            pltpu.make_async_copy(*grads_in).wait()
            pltpu.make_async_copy(*memory_in).wait()
            for t in range(tile_count):
                lanes = slice(t * TILE, (t + 1) * TILE)
                rate = rate_ref[i * tile_count + t]
                mixed = (rate + (1.0 - filter_rate)) * memory_ref[i, :, lanes].astype(jnp.float32)
                mixed = mixed + rate * grads_ref[i, :, lanes].astype(jnp.float32)
                out_ref[i, :, lanes] = mixed.astype(out_ref.dtype)
            pltpu.make_async_copy(*out).start()

    own_half = pltpu.make_async_copy(packed_ref.at[:, :, core], mine, s0.at[0])
    own_half.start()

    @pl.loop(0, slabs)
    def _(i):
        grads_in, memory_in, _ = moves(i)
        pltpu.make_async_copy(*grads_in).start()
        pltpu.make_async_copy(*memory_in).start()

    weights = state_ref[0]
    stat_own[...] = jnp.zeros_like(stat_own)
    for l in range(layers):
        stat_own[l:l + 1, :] = jnp.sum(member_ref[l] * (weights * weights), axis=0, keepdims=True)
    pl.semaphore_wait(barrier, len(peers))

    order = (3, 1, 2, 0)
    reach = sorted(range(1, depth), key=lambda dz: min(dz, depth - dz))
    targets = [(dz, lax.rem(z + dz, depth)) for dz in reach[::-1]] + [(0, z)]
    first_hop, second_hop, third_hop = {}, {}, {}
    for dz, at in targets:
        for dq in order:
            slot = dz * 4 + dq
            first_hop[slot] = copy(packed_ref.at[at, plane(dq), 1 - core], recv1.at[slot],
                                   s1.at[slot], r1.at[slot], device(0, 0, 1))
            first_hop[slot].start()
    own_half.wait()
    for dz, at in targets:
        for dq in order[:3]:
            slot, place = dz * 4 + dq, dz * 3 + dq - 1
            first_hop[slot].wait_recv()
            send2[place] = mine[at, plane(dq)] + recv1[slot]
            second_hop[place] = copy(send2.at[place], recv2.at[place], s2.at[place], r2.at[place], device(0, dq, 0))
            second_hop[place].start()
    filter_slabs(0, slabs // 2)
    here = plane(0)
    summed = None
    for dz, at in targets:
        first_hop[dz * 4].wait_recv()
        for dq in range(3):
            second_hop[dz * 3 + dq].wait_recv()
        part = (mine[at, here] + recv1[dz * 4]) + ((recv2[dz * 3] + recv2[dz * 3 + 1]) + recv2[dz * 3 + 2])
        if dz == 0:
            summed = part
        else:
            send3[dz - 1] = part
            third_hop[dz] = copy(send3.at[dz - 1], recv3.at[dz - 1], s3.at[dz - 1], r3.at[dz - 1], device(dz, 0, 0))
            third_hop[dz].start()
    filter_slabs(slabs // 2, slabs - slabs // 4)
    for dz in range(1, depth):
        third_hop[dz].wait_recv()
        summed = summed + recv3[dz - 1]

    first_sel = beta_one * state_ref[1] + (1.0 - beta_one) * summed
    second_sel = beta_two * state_ref[2] + (1.0 - beta_two) * summed * summed
    update = first_sel / (jnp.sqrt(second_sel) + adam_eps) + weight_decay * weights
    rows_ref[1] = first_sel
    rows_ref[2] = second_sel
    for l in range(layers):
        stat_own[layers + l:layers + l + 1, :] = jnp.sum(member_ref[l] * (update * update), axis=0, keepdims=True)
    def spot(dq, dc):
        return plane(dq) * 2 + xor_bit(core, dc)

    near, away, ahead = [], [], {}
    for i in range(1, 8):
        near.append(copy(stat_own, stat_in.at[spot(0, 0)], s4.at[i - 1], r4.at[i - 1], device(0, i // 2, i % 2)))
        near[-1].start()
    updates[0] = update

    def lift(dz, dq, to_z, to_q, send, at):
        hop = copy(updates.at[at], updates.at[dz * 4 + dq], send, ru.at[dz * 4 + dq], device(to_z, to_q, 0))
        hop.start()
        ahead[dz * 4 + dq] = hop

    for dz in range(1, depth):
        lift(dz, 0, dz, 0, sz.at[dz - 1], 0)
    for dq in order[:3]:
        lift(0, dq, 0, dq, sp.at[dq - 1], 0)
    stat_in[spot(0, 0)] = stat_own[...]
    for i in range(1, 8):
        slot = stat_in.at[spot(i // 2, i % 2)]
        copy(stat_own, slot, s4.at[i - 1], r4.at[i - 1], device(0, i // 2, i % 2)).wait_recv()
    total = stat_in[0]
    for i in range(1, 8):
        total = total + stat_in[i]
    stat_mid[...] = total
    for dz in range(1, depth):
        away.append(copy(stat_mid, stat_far.at[z], s5.at[dz - 1], r5.at[dz - 1], device(dz, 0, 0)))
        away[-1].start()
    stat_far[z] = total
    for dz in reach:
        ahead[dz * 4].wait_recv()
        for dq in order[:3]:
            lift(dz, dq, 0, dq, sp.at[dz * 3 + dq - 1], dz * 4)
    filter_slabs(slabs - slabs // 4, slabs)
    for dz in range(1, depth):
        slot = stat_far.at[lax.rem(z + depth - dz, depth)]
        copy(stat_mid, slot, s5.at[dz - 1], r5.at[dz - 1], device(dz, 0, 0)).wait_recv()
    total = stat_far[0]
    for at in range(1, depth):
        total = total + stat_far[at]
    sums = jnp.sum(total, axis=1, keepdims=True)
    factor = jnp.zeros_like(update)
    for l in range(layers):
        ratio = jnp.sqrt(sums[l:l + 1] / (sums[layers + l:layers + l + 1] + norm_eps))
        factor = factor + member_ref[l] * ratio

    def place(dz, dq):
        scaled = factor * updates[dz * 4 + dq]
        owner = device(dz, dq, 0, back=True)
        for j in range(pieces):
            lanes = pl.ds(pl.multiple_of(owner * entries + j * TILE, TILE), TILE)
            step_ref[:, lanes] = scaled[j * count:(j + 1) * count].astype(step_ref.dtype)

    def chunk(dz, dq, dc):
        return step_ref.at[:, pl.ds(pl.multiple_of(device(dz, dq, dc, back=True) * entries, TILE), entries)]

    started = near + away + [
        hop for hops in (ahead, first_hop, second_hop, third_hop) for hop in hops.values()]
    reached = [0] + reach
    for dz, dq in [(dz, 0) for dz in reached] + [(dz, dq) for dz in reached for dq in (1, 2, 3)]:
        if dq:
            ahead[dz * 4 + dq].wait_recv()
        place(dz, dq)
        block = chunk(dz, dq, 0)
        started.append(copy(block, block, sc.at[dz * 4 + dq], rg.at[dz * 4 + dq], device(0, 0, 1)))
        started[-1].start()
    rows_ref[0] = weights - learn_rate * (factor * update)

    @pl.loop(0, slabs)
    def _(i):
        pltpu.make_async_copy(*moves(i)[2]).wait()

    for dz, dq in [(dz, dq) for dz in reached for dq in range(4)]:
        block = chunk(dz, dq, 1)
        copy(block, block, sc.at[dz * 4 + dq], rg.at[dz * 4 + dq], device(0, 0, 1)).wait_recv()
    for hop in started:
        hop.wait_send()


def state_kernel(layers_smem, blocks_smem, rows_ref, step_hbm, kept_hbm, master_hbm, first_hbm, second_hbm,
                 master_out, first_out, second_out, step_out, kept_out,
                 old_ref, step_ref, kept_ref, in_sem, out_sem, slab_sem, *, layer_rows):
    count = layers_smem.shape[0]
    pieces = rows_ref.shape[1] // count
    slabs = kept_ref.shape[0]
    tile_count = slabs // kept_hbm.shape[0]
    olds, news = [], []
    for s, (source, target) in enumerate(
            ((master_hbm, master_out), (first_hbm, first_out), (second_hbm, second_out))):
        olds.append(pltpu.make_async_copy(source, old_ref.at[s], in_sem.at[s]))
        news.append(pltpu.make_async_copy(old_ref.at[s], target, out_sem.at[s]))
    olds.append(pltpu.make_async_copy(step_hbm, step_ref, in_sem.at[3]))
    news.append(pltpu.make_async_copy(step_ref, step_out, out_sem.at[3]))
    for old in olds:
        old.start()

    def slab(i, hbm):
        rows = pl.ds(pl.multiple_of(lax.rem(i, tile_count) * TILE, TILE), TILE)
        return hbm.at[lax.div(i, tile_count), rows]

    def coming(i):
        return pltpu.make_async_copy(slab(i, kept_hbm), kept_ref.at[i], slab_sem.at[i])

    def going(i):
        return pltpu.make_async_copy(kept_ref.at[i], slab(i, kept_out), slab_sem.at[slabs + i])

    @pl.loop(0, slabs)
    def _(i):
        coming(i).start()

    for s in range(3):
        olds[s].wait()
        for k in range(count):
            column = layers_smem[k] * layer_rows + blocks_smem[k]
            base = pl.ds(pl.multiple_of(lax.div(column, 8) * 8, 8), 8)
            hit = lax.broadcasted_iota(jnp.int32, (8, TILE), 0) == lax.rem(column, 8)
            for j in range(pieces):
                lanes = slice(j * TILE, (j + 1) * TILE)
                line = rows_ref[s, j * count + k:j * count + k + 1, :]
                old_ref[s, base, lanes] = jnp.where(hit, line, old_ref[s, base, lanes])
        news[s].start()
    olds[3].wait()
    news[3].start()

    @pl.loop(0, slabs)
    def _(i):
        coming(i).wait()
        going(i).start()

    @pl.loop(0, slabs)
    def _(i):
        going(i).wait()

    for new in news:
        new.wait()


def on_device_kernels(n, grads, memory, block_ids, layer_ids, master, first_moment, second_moment):
    layers, width, _ = grads.shape
    tile_count = width // TILE
    count = block_ids.shape[0]
    entries = master.shape[1]
    lines = entries // TILE * count
    depth = n // 8
    f32 = jnp.float32
    vmem, smem, hbm = (pl.BlockSpec(memory_space=m) for m in (pltpu.VMEM, pltpu.SMEM, pl.ANY))
    slabs = layers * tile_count
    dma = pltpu.SemaphoreType.DMA
    slab = pltpu.VMEM((slabs, TILE, width), jnp.bfloat16)
    packed, state, member, rates = pl.pallas_call(
        pack_kernel,
        in_specs=[smem, smem] + [hbm] * 5,
        out_specs=[hbm] + [vmem] * 2 + [smem],
        out_shape=[
            jax.ShapeDtypeStruct((n * lines, TILE), f32),
            jax.ShapeDtypeStruct((3, lines, TILE), f32),
            jax.ShapeDtypeStruct((layers, lines, TILE), f32),
            jax.ShapeDtypeStruct((slabs * tile_count,), f32)],
        scratch_shapes=[
            pltpu.VMEM((count, TILE, TILE), jnp.bfloat16),
            pltpu.VMEM((count, TILE, TILE), jnp.bfloat16),
            pltpu.VMEM((n * lines, TILE), f32),
            pltpu.VMEM((3,) + master.shape, f32),
            dma((2 * count,)), dma((3,)), dma((1,))],
        name="pack",
    )(layer_ids, block_ids, grads, memory, master, first_moment, second_moment)
    stat_rows = -(-2 * layers // 8) * 8
    rows, gathered, kept = pl.pallas_call(
        functools.partial(exchange_kernel, n),
        out_shape=[jax.ShapeDtypeStruct((3, lines, TILE), f32),
                   jax.ShapeDtypeStruct((count, n * entries), jnp.bfloat16),
                   jax.ShapeDtypeStruct(memory.shape, jnp.bfloat16)],
        in_specs=[hbm, vmem, vmem, smem, hbm, hbm],
        out_specs=[vmem, vmem, hbm],
        scratch_shapes=[
            pltpu.VMEM((depth, 4, lines, TILE), f32),
            pltpu.VMEM((depth * 4, lines, TILE), f32),
            pltpu.VMEM((depth * 3, lines, TILE), f32),
            pltpu.VMEM((depth * 3, lines, TILE), f32),
            pltpu.VMEM((depth - 1, lines, TILE), f32),
            pltpu.VMEM((depth - 1, lines, TILE), f32),
            pltpu.VMEM((stat_rows, TILE), f32),
            pltpu.VMEM((8, stat_rows, TILE), f32),
            pltpu.VMEM((stat_rows, TILE), f32),
            pltpu.VMEM((depth, stat_rows, TILE), f32),
            pltpu.VMEM((depth * 4, lines, TILE), f32),
            slab, slab, slab,
            dma((1,)), dma((depth * 4,)), dma((depth * 4,)), dma((depth * 3,)), dma((depth * 3,)), dma((depth - 1,)), dma((depth - 1,)),
            dma((7,)), dma((7,)), dma((depth - 1,)), dma((depth - 1,)),
            dma((depth - 1,)), dma((depth * 3,)), dma((depth * 4,)), dma((depth * 4,)), dma((depth * 4,)),
            dma((slabs,)), dma((slabs,)), dma((slabs,))],
        compiler_params=pltpu.CompilerParams(collective_id=0, has_side_effects=True),
        name="exchange",
    )(packed.reshape(depth, 4, 2, lines, TILE), state, member, rates, grads, memory)
    like = jax.ShapeDtypeStruct(master.shape, f32)
    master_new, first_new, second_new, step_blocks, new_memory = pl.pallas_call(
        functools.partial(state_kernel, layer_rows=tile_count * tile_count),
        out_shape=[like] * 3 + [jax.ShapeDtypeStruct(gathered.shape, jnp.bfloat16),
                                jax.ShapeDtypeStruct(memory.shape, jnp.bfloat16)],
        in_specs=[smem, smem, vmem] + [hbm] * 5,
        out_specs=[hbm] * 5,
        scratch_shapes=[pltpu.VMEM((3,) + master.shape, f32), pltpu.VMEM(gathered.shape, jnp.bfloat16), slab,
                        dma((4,)), dma((4,)), dma((2 * slabs,))],
        name="state",
    )(layer_ids, block_ids, rows, gathered, kept, master, first_moment, second_moment)
    return (new_memory, master_new, first_new, second_new, step_blocks)


def solution(mesh):
    n = mesh.shape["dp"]

    def body(*args):
        entries, count = args[4].shape[1], args[2].shape[0]
        if n % 8 == 0 and n > 8 and entries % TILE == 0 and count % 16 == 0:
            return on_device_kernels(n, *args)
        return on_device(*args)

    in_specs = (
        P("dp", None, None),
        P("dp", None, None),
        P(),
        P(),
        P(None, "dp"),
        P(None, "dp"),
        P(None, "dp"),
    )
    out_specs = (P("dp", None, None), P(None, "dp"), P(None, "dp"), P(None, "dp"), P())
    return jax.shard_map(
        body, mesh=mesh, in_specs=in_specs, out_specs=out_specs, check_vma=False
    )
```

```python
import functools

import jax
import jax.numpy as jnp
from jax import lax
from jax.experimental import pallas as pl
from jax.experimental.pallas import tpu as pltpu
from jax.sharding import PartitionSpec as P

TILE = 128


filter_rate = 0.3
beta_one = 0.9
beta_two = 0.999
adam_eps = 1e-06
weight_decay = 0.01
learn_rate = 0.01
norm_eps = 1e-06


def take_tiles(source, layer_ids, tile_row, tile_col):

    def single(layer_id, row_tile, col_tile):
        return lax.dynamic_slice(
            source, (layer_id, row_tile * TILE, col_tile * TILE), (1, TILE, TILE)
        )[0]

    return jax.vmap(single)(layer_ids, tile_row, tile_col)


def pack_blocks(grads_dev, memory_dev, layer_ids, tile_row, tile_col):
    grad_tiles = take_tiles(grads_dev, layer_ids, tile_row, tile_col).astype(jnp.float32)
    memory_tiles = take_tiles(memory_dev, layer_ids, tile_row, tile_col).astype(jnp.float32)
    combined = grad_tiles + memory_tiles
    return combined.reshape(combined.shape[0], TILE * TILE)


def selected_mask(layer_ids, block_ids, layers, tile_count):
    columns = layer_ids * (tile_count * tile_count) + block_ids
    all_columns = jnp.arange(layers * tile_count * tile_count, dtype=jnp.int32)
    chosen = jnp.any(columns[:, None] == all_columns[None, :], axis=0)
    return chosen.reshape(layers, tile_count, 1, tile_count, 1)


def filter_memory(grads_dev, memory_dev, chosen):
    layers, model_width, _ = grads_dev.shape
    tile_count = model_width // TILE
    accumulated = grads_dev.astype(jnp.float32) + memory_dev.astype(jnp.float32)
    shaped = accumulated.reshape(layers, tile_count, TILE, tile_count, TILE)
    filtered = jnp.where(chosen, jnp.float32(0.0), shaped).reshape(layers, model_width, model_width)
    mixed = (1.0 - filter_rate) * memory_dev.astype(jnp.float32) + filter_rate * filtered
    return mixed.astype(jnp.bfloat16)


def adam_rows(summed, weights_sel, first_old, second_old):
    first_sel = beta_one * first_old + (1.0 - beta_one) * summed
    second_sel = beta_two * second_old + (1.0 - beta_two) * summed * summed
    update = first_sel / (jnp.sqrt(second_sel) + adam_eps) + weight_decay * weights_sel
    return (first_sel, second_sel, update)


def layer_squares(member, values):
    return jnp.sum(member * jnp.sum(values * values, axis=1)[:, None], axis=0)


def trust_rows(member, weight_total, update_total):
    trust_ratio = jnp.sqrt(weight_total / (update_total + norm_eps))
    return jnp.sum(member * trust_ratio[None, :], axis=1)


def on_device(grads, memory, block_ids, layer_ids, master, first_moment, second_moment):
    layers, model_width, _ = grads.shape
    tile_count = model_width // TILE
    tile_row = block_ids // tile_count
    tile_col = block_ids % tile_count
    columns = layer_ids * (tile_count * tile_count) + block_ids
    member = (layer_ids[:, None] == jnp.arange(layers, dtype=jnp.int32)[None, :]).astype(
        jnp.float32
    )
    weights_sel = jnp.take(master, columns, axis=0)
    first_old = jnp.take(first_moment, columns, axis=0)
    second_old = jnp.take(second_moment, columns, axis=0)
    packed = pack_blocks(grads, memory, layer_ids, tile_row, tile_col)
    summed = lax.psum_scatter(packed, "dp", scatter_dimension=1, tiled=True)
    first_sel, second_sel, update = adam_rows(summed, weights_sel, first_old, second_old)
    weight_total, update_total = lax.psum(
        (layer_squares(member, weights_sel), layer_squares(member, update)), "dp"
    )
    scaled = trust_rows(member, weight_total, update_total)[:, None] * update
    step_blocks = lax.all_gather(scaled.astype(jnp.bfloat16), "dp", axis=1, tiled=True)
    new_memory = filter_memory(
        grads, memory, selected_mask(layer_ids, block_ids, layers, tile_count)
    )
    master_new = master.at[columns].set(weights_sel - learn_rate * scaled)
    first_new = first_moment.at[columns].set(first_sel)
    second_new = second_moment.at[columns].set(second_sel)
    return (new_memory, master_new, first_new, second_new, step_blocks)


def xor_bit(bit, flip):
    return bit if flip == 0 else 1 - bit


def pack_kernel(layers_smem, blocks_smem, grads_hbm, memory_hbm, master_hbm, first_hbm, second_hbm,
                packed_hbm, state_ref, member_ref, rate_ref,
                grad_tiles, memory_tiles, packed_ref, old_ref, tile_sem, old_sem, packed_sem):
    count = layers_smem.shape[0]
    layers = member_ref.shape[0]
    pieces = state_ref.shape[1] // count
    blocks = rate_ref.shape[0]
    layer_tiles = blocks // layers
    tile_count = grads_hbm.shape[1] // TILE

    tiles = []
    for k in range(count):
        block = blocks_smem[k]
        rows = pl.ds(pl.multiple_of(lax.div(block, tile_count) * TILE, TILE), TILE)
        lanes = pl.ds(pl.multiple_of(lax.rem(block, tile_count) * TILE, TILE), TILE)
        for s, (source, held) in enumerate(((grads_hbm, grad_tiles), (memory_hbm, memory_tiles))):
            tiles.append(pltpu.make_async_copy(
                source.at[layers_smem[k], rows, lanes], held.at[k], tile_sem.at[s * count + k]))
            tiles[-1].start()
    olds = []
    for s, source in enumerate((master_hbm, first_hbm, second_hbm)):
        olds.append(pltpu.make_async_copy(source, old_ref.at[s], old_sem.at[s]))
        olds[-1].start()

    for t in range(blocks):
        rate_ref[t] = jnp.float32(filter_rate)
    for k in range(count):
        rate_ref[layers_smem[k] * layer_tiles + blocks_smem[k]] = jnp.float32(0.0)
        for l in range(layers):
            flag = jnp.where(layers_smem[k] == l, jnp.float32(1.0), jnp.float32(0.0))
            for j in range(pieces):
                member_ref[l, j * count + k:j * count + k + 1, :] = jnp.full((1, TILE), flag, jnp.float32)
    for k in range(count):
        tiles[2 * k].wait()
        tiles[2 * k + 1].wait()
        packed_ref[pl.ds(k, TILE, stride=count), :] = (
            grad_tiles[k].astype(jnp.float32) + memory_tiles[k].astype(jnp.float32))
    packed_out = pltpu.make_async_copy(packed_ref, packed_hbm, packed_sem.at[0])
    packed_out.start()
    for old in olds:
        old.wait()
    for k in range(count):
        column = layers_smem[k] * layer_tiles + blocks_smem[k]
        for s in range(3):
            line = old_ref[s, pl.ds(column, 1), :]
            for j in range(pieces):
                state_ref[s, j * count + k:j * count + k + 1, :] = line[:, j * TILE:(j + 1) * TILE]
    packed_out.wait()


def exchange_kernel(n, packed_ref, state_ref, member_ref, rate_ref, grads_hbm, memory_hbm, rows_ref, step_ref, out_hbm,
                    mine, recv1, send2, recv2, send3, recv3, stat_own, stat_in, stat_mid, stat_far, updates, grads_ref, memory_ref, out_ref,
                    s0, s1, r1, s2, r2, s3, r3, s4, r4, s5, r5, sz, sp, ru, sc, rg,
                    grads_sem, memory_sem, out_sem):
    depth = n // 8
    layers = member_ref.shape[0]
    count = step_ref.shape[0]
    entries = step_ref.shape[1] // n
    pieces = entries // TILE
    me = lax.axis_index("dp")
    core = lax.rem(me, 2)
    x = lax.rem(lax.div(me, 2), 2)
    y = lax.rem(lax.div(me, 4), 2)
    z = lax.div(me, 8)

    def device(dz, dq, dc, back=False):
        far = lax.rem(z + (depth - dz if back else dz), depth) if dz else z
        return far * 8 + xor_bit(y, dq // 2) * 4 + xor_bit(x, dq % 2) * 2 + xor_bit(core, dc)

    def plane(dq):
        return xor_bit(y, dq // 2) * 2 + xor_bit(x, dq % 2)

    def copy(src, dst, send, recv, peer):
        return pltpu.make_async_remote_copy(
            src_ref=src, dst_ref=dst, send_sem=send, recv_sem=recv,
            device_id=(peer,), device_id_type=pl.DeviceIdType.MESH)

    barrier = pltpu.get_barrier_semaphore()
    peers = [device(0, i // 2, i % 2) for i in range(1, 8)] + [device(dz, 0, 0) for dz in range(1, depth)]
    for peer in peers:
        pl.semaphore_signal(barrier, inc=1, device_id=(peer,), device_id_type=pl.DeviceIdType.MESH)
    slabs = grads_ref.shape[0]
    tile_count = slabs // layers

    def moves(i):
        layer, rows = lax.div(i, tile_count), pl.ds(pl.multiple_of(lax.rem(i, tile_count) * TILE, TILE), TILE)
        return ((grads_hbm.at[layer, rows], grads_ref.at[i], grads_sem.at[i]),
                (memory_hbm.at[layer, rows], memory_ref.at[i], memory_sem.at[i]),
                (out_ref.at[i], out_hbm.at[layer, rows], out_sem.at[i]))

    def filter_slabs(start, stop):
        @pl.loop(start, stop)
        def _(i):
            grads_in, memory_in, out = moves(i)
            pltpu.make_async_copy(*grads_in).wait()
            pltpu.make_async_copy(*memory_in).wait()
            for t in range(tile_count):
                lanes = slice(t * TILE, (t + 1) * TILE)
                rate = rate_ref[i * tile_count + t]
                mixed = (rate + (1.0 - filter_rate)) * memory_ref[i, :, lanes].astype(jnp.float32)
                mixed = mixed + rate * grads_ref[i, :, lanes].astype(jnp.float32)
                out_ref[i, :, lanes] = mixed.astype(out_ref.dtype)
            pltpu.make_async_copy(*out).start()

    own_half = pltpu.make_async_copy(packed_ref.at[:, :, core], mine, s0.at[0])
    own_half.start()
    weights = state_ref[0]
    stat_own[...] = jnp.zeros_like(stat_own)
    for l in range(layers):
        stat_own[l:l + 1, :] = jnp.sum(member_ref[l] * (weights * weights), axis=0, keepdims=True)
    pl.semaphore_wait(barrier, len(peers))

    order = (3, 1, 2, 0)
    reach = sorted(range(1, depth), key=lambda dz: min(dz, depth - dz))
    targets = [(dz, lax.rem(z + dz, depth)) for dz in reach[::-1]] + [(0, z)]
    first_hop, second_hop, third_hop = {}, {}, {}
    for dz, at in targets:
        for dq in order:
            slot = dz * 4 + dq
            first_hop[slot] = copy(packed_ref.at[at, plane(dq), 1 - core], recv1.at[slot],
                                   s1.at[slot], r1.at[slot], device(0, 0, 1))
            first_hop[slot].start()
    own_half.wait()

    @pl.loop(0, slabs)
    def _(i):
        grads_in, memory_in, _ = moves(i)
        pltpu.make_async_copy(*grads_in).start()
        pltpu.make_async_copy(*memory_in).start()

    for dz, at in targets:
        for dq in order[:3]:
            slot, place = dz * 4 + dq, dz * 3 + dq - 1
            first_hop[slot].wait_recv()
            send2[place] = mine[at, plane(dq)] + recv1[slot]
            second_hop[place] = copy(send2.at[place], recv2.at[place], s2.at[place], r2.at[place], device(0, dq, 0))
            second_hop[place].start()
    filter_slabs(0, slabs // 2)
    here = plane(0)
    summed = None
    for dz, at in targets:
        first_hop[dz * 4].wait_recv()
        for dq in range(3):
            second_hop[dz * 3 + dq].wait_recv()
        part = (mine[at, here] + recv1[dz * 4]) + ((recv2[dz * 3] + recv2[dz * 3 + 1]) + recv2[dz * 3 + 2])
        if dz == 0:
            summed = part
        else:
            send3[dz - 1] = part
            third_hop[dz] = copy(send3.at[dz - 1], recv3.at[dz - 1], s3.at[dz - 1], r3.at[dz - 1], device(dz, 0, 0))
            third_hop[dz].start()
    filter_slabs(slabs // 2, slabs - slabs // 4)
    for dz in range(1, depth):
        third_hop[dz].wait_recv()
        summed = summed + recv3[dz - 1]

    first_sel = beta_one * state_ref[1] + (1.0 - beta_one) * summed
    second_sel = beta_two * state_ref[2] + (1.0 - beta_two) * summed * summed
    update = first_sel / (jnp.sqrt(second_sel) + adam_eps) + weight_decay * weights
    rows_ref[1] = first_sel
    rows_ref[2] = second_sel
    for l in range(layers):
        stat_own[layers + l:layers + l + 1, :] = jnp.sum(member_ref[l] * (update * update), axis=0, keepdims=True)
    def spot(dq, dc):
        return plane(dq) * 2 + xor_bit(core, dc)

    near, away, ahead = [], [], {}
    for i in range(1, 8):
        near.append(copy(stat_own, stat_in.at[spot(0, 0)], s4.at[i - 1], r4.at[i - 1], device(0, i // 2, i % 2)))
        near[-1].start()
    updates[0] = update

    def lift(dz, dq, to_z, to_q, send, at):
        hop = copy(updates.at[at], updates.at[dz * 4 + dq], send, ru.at[dz * 4 + dq], device(to_z, to_q, 0))
        hop.start()
        ahead[dz * 4 + dq] = hop

    for dz in range(1, depth):
        lift(dz, 0, dz, 0, sz.at[dz - 1], 0)
    for dq in order[:3]:
        lift(0, dq, 0, dq, sp.at[dq - 1], 0)
    stat_in[spot(0, 0)] = stat_own[...]
    for i in range(1, 8):
        slot = stat_in.at[spot(i // 2, i % 2)]
        copy(stat_own, slot, s4.at[i - 1], r4.at[i - 1], device(0, i // 2, i % 2)).wait_recv()
    total = stat_in[0]
    for i in range(1, 8):
        total = total + stat_in[i]
    stat_mid[...] = total
    for dz in range(1, depth):
        away.append(copy(stat_mid, stat_far.at[z], s5.at[dz - 1], r5.at[dz - 1], device(dz, 0, 0)))
        away[-1].start()
    stat_far[z] = total
    for dz in reach:
        ahead[dz * 4].wait_recv()
        for dq in order[:3]:
            lift(dz, dq, 0, dq, sp.at[dz * 3 + dq - 1], dz * 4)
    filter_slabs(slabs - slabs // 4, slabs)
    for dz in range(1, depth):
        slot = stat_far.at[lax.rem(z + depth - dz, depth)]
        copy(stat_mid, slot, s5.at[dz - 1], r5.at[dz - 1], device(dz, 0, 0)).wait_recv()
    total = stat_far[0]
    for at in range(1, depth):
        total = total + stat_far[at]
    sums = jnp.sum(total, axis=1, keepdims=True)
    factor = jnp.zeros_like(update)
    for l in range(layers):
        ratio = jnp.sqrt(sums[l:l + 1] / (sums[layers + l:layers + l + 1] + norm_eps))
        factor = factor + member_ref[l] * ratio

    def place(dz, dq):
        scaled = factor * updates[dz * 4 + dq]
        owner = device(dz, dq, 0, back=True)
        for j in range(pieces):
            lanes = pl.ds(pl.multiple_of(owner * entries + j * TILE, TILE), TILE)
            step_ref[:, lanes] = scaled[j * count:(j + 1) * count].astype(step_ref.dtype)

    def chunk(dz, dq, dc):
        return step_ref.at[:, pl.ds(pl.multiple_of(device(dz, dq, dc, back=True) * entries, TILE), entries)]

    started = near + away + [
        hop for hops in (ahead, first_hop, second_hop, third_hop) for hop in hops.values()]
    reached = [0] + reach
    for dz, dq in [(dz, 0) for dz in reached] + [(dz, dq) for dz in reached for dq in (1, 2, 3)]:
        if dq:
            ahead[dz * 4 + dq].wait_recv()
        place(dz, dq)
        block = chunk(dz, dq, 0)
        started.append(copy(block, block, sc.at[dz * 4 + dq], rg.at[dz * 4 + dq], device(0, 0, 1)))
        started[-1].start()
    rows_ref[0] = weights - learn_rate * (factor * update)

    @pl.loop(0, slabs)
    def _(i):
        pltpu.make_async_copy(*moves(i)[2]).wait()

    for dz, dq in [(dz, dq) for dz in reached for dq in range(4)]:
        block = chunk(dz, dq, 1)
        copy(block, block, sc.at[dz * 4 + dq], rg.at[dz * 4 + dq], device(0, 0, 1)).wait_recv()
    for hop in started:
        hop.wait_send()


def state_kernel(layers_smem, blocks_smem, rows_ref, step_hbm, kept_hbm, master_hbm, first_hbm, second_hbm,
                 master_out, first_out, second_out, step_out, kept_out,
                 old_ref, step_ref, kept_ref, in_sem, out_sem, slab_sem, *, layer_rows):
    count = layers_smem.shape[0]
    pieces = rows_ref.shape[1] // count
    slabs = kept_ref.shape[0]
    tile_count = slabs // kept_hbm.shape[0]
    olds, news = [], []
    for s, (source, target) in enumerate(
            ((master_hbm, master_out), (first_hbm, first_out), (second_hbm, second_out))):
        olds.append(pltpu.make_async_copy(source, old_ref.at[s], in_sem.at[s]))
        news.append(pltpu.make_async_copy(old_ref.at[s], target, out_sem.at[s]))
    olds.append(pltpu.make_async_copy(step_hbm, step_ref, in_sem.at[3]))
    news.append(pltpu.make_async_copy(step_ref, step_out, out_sem.at[3]))
    for old in olds:
        old.start()

    def slab(i, hbm):
        rows = pl.ds(pl.multiple_of(lax.rem(i, tile_count) * TILE, TILE), TILE)
        return hbm.at[lax.div(i, tile_count), rows]

    def coming(i):
        return pltpu.make_async_copy(slab(i, kept_hbm), kept_ref.at[i], slab_sem.at[i])

    def going(i):
        return pltpu.make_async_copy(kept_ref.at[i], slab(i, kept_out), slab_sem.at[slabs + i])

    @pl.loop(0, slabs)
    def _(i):
        coming(i).start()

    for s in range(3):
        olds[s].wait()
        for k in range(count):
            column = layers_smem[k] * layer_rows + blocks_smem[k]
            base = pl.ds(pl.multiple_of(lax.div(column, 8) * 8, 8), 8)
            hit = lax.broadcasted_iota(jnp.int32, (8, TILE), 0) == lax.rem(column, 8)
            for j in range(pieces):
                lanes = slice(j * TILE, (j + 1) * TILE)
                line = rows_ref[s, j * count + k:j * count + k + 1, :]
                old_ref[s, base, lanes] = jnp.where(hit, line, old_ref[s, base, lanes])
        news[s].start()
    olds[3].wait()
    news[3].start()

    @pl.loop(0, slabs)
    def _(i):
        coming(i).wait()
        going(i).start()

    @pl.loop(0, slabs)
    def _(i):
        going(i).wait()

    for new in news:
        new.wait()


def on_device_kernels(n, grads, memory, block_ids, layer_ids, master, first_moment, second_moment):
    layers, width, _ = grads.shape
    tile_count = width // TILE
    count = block_ids.shape[0]
    entries = master.shape[1]
    lines = entries // TILE * count
    depth = n // 8
    f32 = jnp.float32
    vmem, smem, hbm = (pl.BlockSpec(memory_space=m) for m in (pltpu.VMEM, pltpu.SMEM, pl.ANY))
    slabs = layers * tile_count
    dma = pltpu.SemaphoreType.DMA
    slab = pltpu.VMEM((slabs, TILE, width), jnp.bfloat16)
    packed, state, member, rates = pl.pallas_call(
        pack_kernel,
        in_specs=[smem, smem] + [hbm] * 5,
        out_specs=[hbm] + [vmem] * 2 + [smem],
        out_shape=[
            jax.ShapeDtypeStruct((n * lines, TILE), f32),
            jax.ShapeDtypeStruct((3, lines, TILE), f32),
            jax.ShapeDtypeStruct((layers, lines, TILE), f32),
            jax.ShapeDtypeStruct((slabs * tile_count,), f32)],
        scratch_shapes=[
            pltpu.VMEM((count, TILE, TILE), jnp.bfloat16),
            pltpu.VMEM((count, TILE, TILE), jnp.bfloat16),
            pltpu.VMEM((n * lines, TILE), f32),
            pltpu.VMEM((3,) + master.shape, f32),
            dma((2 * count,)), dma((3,)), dma((1,))],
        name="pack",
    )(layer_ids, block_ids, grads, memory, master, first_moment, second_moment)
    stat_rows = -(-2 * layers // 8) * 8
    rows, gathered, kept = pl.pallas_call(
        functools.partial(exchange_kernel, n),
        out_shape=[jax.ShapeDtypeStruct((3, lines, TILE), f32),
                   jax.ShapeDtypeStruct((count, n * entries), jnp.bfloat16),
                   jax.ShapeDtypeStruct(memory.shape, jnp.bfloat16)],
        in_specs=[hbm, vmem, vmem, smem, hbm, hbm],
        out_specs=[vmem, vmem, hbm],
        scratch_shapes=[
            pltpu.VMEM((depth, 4, lines, TILE), f32),
            pltpu.VMEM((depth * 4, lines, TILE), f32),
            pltpu.VMEM((depth * 3, lines, TILE), f32),
            pltpu.VMEM((depth * 3, lines, TILE), f32),
            pltpu.VMEM((depth - 1, lines, TILE), f32),
            pltpu.VMEM((depth - 1, lines, TILE), f32),
            pltpu.VMEM((stat_rows, TILE), f32),
            pltpu.VMEM((8, stat_rows, TILE), f32),
            pltpu.VMEM((stat_rows, TILE), f32),
            pltpu.VMEM((depth, stat_rows, TILE), f32),
            pltpu.VMEM((depth * 4, lines, TILE), f32),
            slab, slab, slab,
            dma((1,)), dma((depth * 4,)), dma((depth * 4,)), dma((depth * 3,)), dma((depth * 3,)), dma((depth - 1,)), dma((depth - 1,)),
            dma((7,)), dma((7,)), dma((depth - 1,)), dma((depth - 1,)),
            dma((depth - 1,)), dma((depth * 3,)), dma((depth * 4,)), dma((depth * 4,)), dma((depth * 4,)),
            dma((slabs,)), dma((slabs,)), dma((slabs,))],
        compiler_params=pltpu.CompilerParams(collective_id=0, has_side_effects=True),
        name="exchange",
    )(packed.reshape(depth, 4, 2, lines, TILE), state, member, rates, grads, memory)
    like = jax.ShapeDtypeStruct(master.shape, f32)
    master_new, first_new, second_new, step_blocks, new_memory = pl.pallas_call(
        functools.partial(state_kernel, layer_rows=tile_count * tile_count),
        out_shape=[like] * 3 + [jax.ShapeDtypeStruct(gathered.shape, jnp.bfloat16),
                                jax.ShapeDtypeStruct(memory.shape, jnp.bfloat16)],
        in_specs=[smem, smem, vmem] + [hbm] * 5,
        out_specs=[hbm] * 5,
        scratch_shapes=[pltpu.VMEM((3,) + master.shape, f32), pltpu.VMEM(gathered.shape, jnp.bfloat16), slab,
                        dma((4,)), dma((4,)), dma((2 * slabs,))],
        name="state",
    )(layer_ids, block_ids, rows, gathered, kept, master, first_moment, second_moment)
    return (new_memory, master_new, first_new, second_new, step_blocks)


def solution(mesh):
    n = mesh.shape["dp"]

    def body(*args):
        entries, count = args[4].shape[1], args[2].shape[0]
        if n % 8 == 0 and n > 8 and entries % TILE == 0 and count % 16 == 0:
            return on_device_kernels(n, *args)
        return on_device(*args)

    in_specs = (
        P("dp", None, None),
        P("dp", None, None),
        P(),
        P(),
        P(None, "dp"),
        P(None, "dp"),
        P(None, "dp"),
    )
    out_specs = (P("dp", None, None), P(None, "dp"), P(None, "dp"), P(None, "dp"), P())
    return jax.shard_map(
        body, mesh=mesh, in_specs=in_specs, out_specs=out_specs, check_vma=False
    )
```
